256 devices in a mesh: req: 32 (over z, y), seq: 8 (over x, core).
Axes of the slice: x: 4, y: 4, z: 8, core: 2. Of those that a mesh axis runs over, the one named last changes fastest.
Arguments:
- tokens: bfloat16 [32, 4096, 2560], P('req', 'seq'), may hold values from -6 to 6
- mix_weight: bfloat16 [2560, 2816], P(('req', 'seq')), may hold values from -0.125 to 0.125
- step_weight: bfloat16 [2560, 40], P(('req', 'seq')), may hold values from -0.125 to 0.125
- conv_weight: float32 [4, 2816], replicated, may hold values from -3 to 3
- conv_bias: float32 [2816], replicated, may hold values from -3 to 3
- step_bias: float32 [40], replicated, may hold values from -5 to -3
- decay_rate: float32 [40], replicated, may hold values from 0.00048828125 to 1
- skip_gain: float32 [40], replicated, may hold values from 0.5 to 2
- norm_gain: float32 [2560], replicated, may hold values from 0.1 to 1.9
- prompt_len: int32 [32], replicated, may hold values from 1024 to 4096, as said below
- prompt_start: int32 [32], replicated, may hold values from 0 to 3072, as said below
- deal: int32 [32], replicated, may hold values from 0 to 31, as said below
Outputs:
- result: bfloat16 [32, 4096, 2560], P('req', 'seq')
- final_state: float32 [32, 40, 64, 128], P('req', 'seq')
The draws below stay inside these ranges and needn't reach their ends.
Inputs may be any that keep to these rules, and one draw needn't show every extreme that they name: `prompt_len`: one prompt has exactly 4096 positions and one exactly a quarter of 4096. prompt_start plus prompt_len is at most 4096 for every request. `deal`: a permutation of the requests; some slot s holds request (s + 16) modulo 32.
All inputs are finite; a program needn't handle non-finite values.
Results may differ from the reference program's by a relative error of at most 0.0035.
Values may be sent and summed in bfloat16 or wider, within the bound.
A program may use at most 128 MiB of HBM per device.

```python
import math
import jax
import jax.numpy as jnp
from jax import lax

D = 2560
HEADS = 40
P_SIZE = 64
NSTATE = 128
CONV = 4
GROUP = 256
E = 2560
CONVCH = 2816
REQS = 32
MAXLEN = 4096


def joint_prompt(key):
    inner_key = jax.random.fold_in(key, 11)
    keys = jax.random.split(inner_key, 4)
    places = jnp.arange(REQS, dtype=jnp.int32)
    lengths = jax.random.randint(keys[0], (REQS,), MAXLEN // 4, MAXLEN + 1)
    longest = jax.random.randint(keys[1], (), 0, REQS)
    shortest = (longest + 1 + jax.random.randint(keys[2], (), 0, REQS - 1)) % REQS
    lengths = jnp.where(places == longest, MAXLEN, lengths)
    lengths = jnp.where(places == shortest, MAXLEN // 4, lengths)
    offsets = jax.random.randint(keys[3], (REQS,), 0, MAXLEN - lengths + 1)
    offsets = jnp.where(places == shortest, MAXLEN - MAXLEN // 4, offsets)
    return (lengths.astype(jnp.int32), offsets.astype(jnp.int32))


def draw_prompt_len(key, part):
    return joint_prompt(key)[0]


def draw_prompt_start(key, part):
    return joint_prompt(key)[1]


def draw_deal(key, part):
    inner_key = jax.random.fold_in(key, 23)
    keys = jax.random.split(inner_key, 2)
    places = jnp.arange(REQS, dtype=jnp.int32)
    order = jax.random.permutation(keys[0], REQS).astype(jnp.int32)
    chosen = jax.random.randint(keys[1], (), 0, REQS).astype(jnp.int32)
    target = (chosen + REQS // 2) % REQS
    holder = jnp.sum(jnp.where(order == target, places, 0))
    current = jnp.sum(jnp.where(places == chosen, order, 0))
    swapped = jnp.where(places == holder, current, order)
    swapped = jnp.where(places == chosen, target, swapped)
    return swapped.astype(jnp.int32)


def levels(rng, extent, cuts, smallest, largest):
    gain, own = 1.0, jax.random.fold_in(rng, 6)
    for position, blocks in cuts:
        draws = jnp.exp(jax.random.uniform(jax.random.fold_in(own, position), (blocks,), jnp.float32, smallest / len(cuts), largest / len(cuts)))
        gain = gain * jnp.repeat(draws, extent[position] // blocks).reshape([-1 if axis == position else 1 for axis in range(len(extent))])
    return gain


def centred(stream_key, extent, deviation, limit, shards=(), kind=jnp.bfloat16):
    values = deviation * jax.random.normal(stream_key, extent, jnp.float32)
    if shards:
        values = values * levels(stream_key, extent, shards, -0.22, 0.18)
    return jnp.clip(values, -limit, limit).astype(kind)


def setup_inputs(seed: int = 0) -> dict:
    seeds = jax.random.split(jax.random.key(seed), 13)
    return {
        "tokens": centred(seeds[0], (REQS, MAXLEN, D), 1.0, 6.0, ((0, 32), (1, 8))),
        "mix_weight": centred(seeds[1], (D, CONVCH), D ** -0.5, 0.125, ((0, 256),)),
        "step_weight": centred(seeds[2], (D, HEADS), D ** -0.5, 0.125, ((0, 256),)),
        "conv_weight": centred(seeds[3], (CONV, CONVCH), 0.5, 3.0, (), jnp.float32),
        "conv_bias": centred(seeds[4], (CONVCH,), 0.5, 3.0, (), jnp.float32),
        "step_bias": jnp.clip(jax.random.uniform(seeds[5], (HEADS,), jnp.float32, -5.0, -3.0), -5.0, -3.0),
        "decay_rate": jnp.clip(jnp.exp(jax.random.uniform(seeds[6], (HEADS,), jnp.float32, math.log(0.00048828125), math.log(1.0))), 0.00048828125, 1.0),
        "skip_gain": jnp.clip(jax.random.uniform(seeds[7], (HEADS,), jnp.float32, 0.5, 2.0), 0.5, 2.0),
        "norm_gain": jnp.clip(1.0 + 0.18 * jax.random.normal(seeds[8], (E,), jnp.float32), 0.1, 1.9),
        "prompt_len": draw_prompt_len(jax.random.fold_in(seeds[12], 71), 0),
        "prompt_start": draw_prompt_start(jax.random.fold_in(seeds[12], 71), 0),
        "deal": draw_deal(jax.random.fold_in(seeds[12], 71), 0),
    }


EPS = 1e-05

def group_step(state, block, decay_rate):
    part_in, part_b, part_c, part_step = block
    log_decay = -part_step * decay_rate[None, :]
    cum_decay = jnp.cumsum(log_decay, axis=0)
    count = part_in.shape[0]
    places = jnp.arange(count, dtype=jnp.int32)
    causal = places[:, None] >= places[None, :]
    spread = cum_decay[:, None, :] - cum_decay[None, :, :]
    spread = jnp.where(causal[:, :, None], spread, -1e+30)
    scores = jnp.dot(part_c, part_b.T, preferred_element_type=jnp.float32)
    mixing = (jnp.exp(spread) * scores[:, :, None] * part_step[None, :, :]).astype(jnp.bfloat16)
    inner_out = jnp.einsum('qkh,khp->qhp', mixing.astype(jnp.float32), part_in.astype(jnp.float32))
    carried = jnp.einsum('qn,hpn->qhp', part_c.astype(jnp.float32), state, precision=lax.Precision.HIGHEST)
    carried = carried * jnp.exp(cum_decay)[:, :, None]
    to_end = jnp.exp(cum_decay[-1][None, :] - cum_decay) * part_step
    scaled = (to_end[:, :, None] * part_in.astype(jnp.float32)).astype(jnp.bfloat16)
    local = jnp.einsum('khp,kn->hpn', scaled.astype(jnp.float32), part_b.astype(jnp.float32))
    new_state = jnp.exp(cum_decay[-1])[:, None, None] * state + local
    return (new_state, inner_out + carried)

def one_row(tokens_row, length, start, mix_weight, step_weight, conv_weight, conv_bias, step_bias, decay_rate, skip_gain, norm_gain):
    total = tokens_row.shape[0]
    place = jnp.arange(total, dtype=jnp.int32)
    valid = ((place >= start) & (place < start + length)).astype(jnp.float32)
    mixed = jnp.dot(tokens_row, mix_weight, preferred_element_type=jnp.float32)
    mixed = (mixed * valid[:, None]).astype(jnp.bfloat16)
    raw_step = jnp.dot(tokens_row, step_weight, preferred_element_type=jnp.float32)
    padded = jnp.concatenate([jnp.zeros((CONV - 1, CONVCH), jnp.bfloat16), mixed], axis=0)
    conv_sum = jnp.zeros((total, CONVCH), jnp.float32) + conv_bias[None, :]
    for offset in range(CONV):
        conv_sum = conv_sum + conv_weight[offset][None, :] * padded[offset:offset + total].astype(jnp.float32)
    convolved = jax.nn.silu(conv_sum).astype(jnp.bfloat16)
    inputs = convolved[:, :E].reshape(total, HEADS, P_SIZE)
    mixed_b = convolved[:, E:E + NSTATE]
    mixed_c = convolved[:, E + NSTATE:]
    step_size = jax.nn.softplus(raw_step + step_bias[None, :]) * valid[:, None]
    blocks = total // GROUP
    pieces = (inputs.reshape(blocks, GROUP, HEADS, P_SIZE), mixed_b.reshape(blocks, GROUP, NSTATE), mixed_c.reshape(blocks, GROUP, NSTATE), step_size.reshape(blocks, GROUP, HEADS))

    def advance(state, block):
        return group_step(state, block, decay_rate)
    final_state, outputs = lax.scan(advance, jnp.zeros((HEADS, P_SIZE, NSTATE), jnp.float32), pieces)
    outputs = outputs.reshape(total, HEADS, P_SIZE) + skip_gain[None, :, None] * inputs.astype(jnp.float32)
    flat = outputs.reshape(total, E)
    factor = lax.rsqrt(lax.optimization_barrier(jnp.mean(flat * flat, axis=1, keepdims=True)) + EPS)
    result = (flat * factor * norm_gain[None, :] * valid[:, None]).astype(jnp.bfloat16)
    return (result, final_state)

def reference(tokens, mix_weight, step_weight, conv_weight, conv_bias, step_bias, decay_rate, skip_gain, norm_gain, prompt_len, prompt_start, deal):
    slot_len = prompt_len[deal]
    slot_start = prompt_start[deal]

    def run(item):
        row, length, start = item
        return one_row(row, length, start, mix_weight, step_weight, conv_weight, conv_bias, step_bias, decay_rate, skip_gain, norm_gain)
    result, states = lax.map(run, (tokens, slot_len, slot_start))
    final_state = jnp.zeros_like(states).at[deal].set(states)
    return (result, final_state)
```

```python
import functools

import jax
import jax.numpy as jnp
from jax import lax
from jax.experimental import pallas as pl
from jax.experimental.pallas import tpu as pltpu
from jax.sharding import PartitionSpec as P

F32, BF16 = jnp.float32, jnp.bfloat16
MESH = pl.DeviceIdType.MESH
HIGH = lax.Precision.HIGHEST
EPS = 1e-05

SPAN = 512
HALO = 16
CH = 128
NCH = SPAN // CH
D = 2560
SLOTS = 12
GROUPS = 10
LAG = 7
DONE_AT = [(5 * d + 4) // 4 for d in range(8)]


def dot(a, b, **kw):
    return jnp.dot(a, b, preferred_element_type=F32, **kw)


def kernel(
    tok_hbm, wl_ref, cw_ref, hv_ref, len_s, start_s, deal_s,
    res_hbm, fin_ref,
    wb, stage, tokv, valid, conv, out, resv, cum, cum_t, step_t, wk, ec, sc, bt, cc,
    dc, dw, ta, lb, dst, d0, tb, tr, ib, fb, zg, ys, yr, ssq,
    w_send, w_recv, h_sem, tok_sem, g_send, g_recv, sib_send, sib_recv,
    t_send, t_recv, d_send, d_recv, x_send, x_recv, i_send, i_recv,
    f_send, f_recv, z_send, z_recv, y_send, y_recv, o_sem,
):
    r, q = lax.axis_index("req"), lax.axis_index("seq")
    z, y, x, c = r // 4, r % 4, q // 2, q % 2
    yn = [(z * 4 + (y + d) % 4, q) for d in range(4)]
    zn = [(((z + d) % 8) * 4 + y, q) for d in range(8)]
    qn = [(r, (q + d) % 8) for d in range(8)]
    yp, ym, zp, zm = yn[1], yn[3], zn[1], zn[7]
    sib = (r, q + 1 - 2 * c)
    yi = [(y + d) % 4 for d in range(4)]
    zi = [(z + d) % 8 for d in range(8)]

    def remote(src, to, ssem, rsem, dev):
        return pltpu.make_async_remote_copy(
            src_ref=src, dst_ref=to, send_sem=ssem, recv_sem=rsem,
            device_id=dev, device_id_type=MESH,
        )

    barrier = pltpu.get_barrier_semaphore()
    partners = qn[1:] + yn[1:] + [zp, zm]
    for dev in partners:
        pl.semaphore_signal(barrier, inc=1, device_id=dev, device_id_type=MESH)
    tok_copy = pltpu.make_async_copy(tok_hbm, tokv.at[pl.ds(HALO, SPAN)], tok_sem)
    tok_copy.start()
    pl.semaphore_wait(barrier, len(partners))

    own_w = pltpu.make_async_copy(wl_ref.at[c], stage.at[q], w_recv.at[7])
    own_w.start()
    w_copies = []
    for d in range(1, 8):
        to = (q + d) % 8
        w_copies.append(
            remote(wl_ref.at[to % 2], stage.at[q], w_send.at[d - 1], w_recv.at[d - 1], qn[d])
        )
        w_copies[-1].start()
    halo = remote(
        tok_hbm.at[pl.ds(SPAN - HALO, HALO)], tokv.at[pl.ds(0, HALO)],
        h_sem.at[0], h_sem.at[1], qn[1],
    )
    halo.start()

    request = deal_s[r]
    first = start_s[request]
    last = first + len_s[request]
    place = lax.broadcasted_iota(jnp.int32, (SPAN + HALO, 128), 0) + (q * SPAN - HALO)
    valid[...] = jnp.where((place >= first) & (place < last), 1.0, 0.0)
    ssq[...] = jnp.zeros_like(ssq)

    own_w.wait()
    for d in range(1, 8):
        src = (q - d) % 8
        remote(
            wl_ref.at[0], stage.at[src], w_send.at[d - 1], w_recv.at[d - 1], qn[d]
        ).wait_recv()
    row = lax.broadcasted_iota(jnp.int32, (80, 128), 0)
    col = lax.broadcasted_iota(jnp.int32, (80, 128), 1)
    pick = jnp.where(col == (row // 10) * 16 + row % 10, 1.0, 0.0).astype(BF16)
    for s in range(SLOTS):
        part = stage[:, :, s * 128 : (s + 1) * 128].reshape(128, 128)
        wb[c, s, z, y] = dot(pick, part).astype(BF16)
    for copy in w_copies:
        copy.wait_send()
    tok_copy.wait()
    halo.wait_send()
    halo.wait_recv()

    def blk(s, dz, dy):
        return wb.at[c, s, zi[dz], yi[dy]]

    def lo(ref):
        return ref.at[pl.ds(0, 48)]

    def hi(ref):
        return ref.at[pl.ds(48, 32)]

    def zset(s, dz):
        return wb.at[0, s, zi[dz]]

    def yset(s, dy):
        return wb.at[1, s, :, yi[dy]]

    def messages(core, s):
        if core == 0:
            return [
                (blk(s, 0, 3), blk(s, 0, 0), yp),
                (blk(s, 0, 1), blk(s, 0, 0), ym),
                (lo(blk(s, 0, 2)), lo(blk(s, 0, 3)), yp),
                (hi(blk(s, 0, 2)), hi(blk(s, 0, 1)), ym),
                (zset(s, 7), zset(s, 0), zp),
                (zset(s, 1), zset(s, 0), zm),
                (zset(s, 6), zset(s, 7), zp),
                (zset(s, 2), zset(s, 1), zm),
                (zset(s, 5), zset(s, 6), zp),
                (zset(s, 3), zset(s, 2), zm),
                (zset(s, 4).at[pl.ds(0, 2)], zset(s, 5).at[pl.ds(0, 2)], zp),
                (zset(s, 4).at[pl.ds(2, 2)], zset(s, 3).at[pl.ds(2, 2)], zm),
            ]
        return [
            (blk(s, 7, 0), blk(s, 0, 0), zp),
            (blk(s, 1, 0), blk(s, 0, 0), zm),
            (blk(s, 6, 0), blk(s, 7, 0), zp),
            (blk(s, 2, 0), blk(s, 1, 0), zm),
            (blk(s, 5, 0), blk(s, 6, 0), zp),
            (blk(s, 3, 0), blk(s, 2, 0), zm),
            (lo(blk(s, 4, 0)), lo(blk(s, 5, 0)), zp),
            (hi(blk(s, 4, 0)), hi(blk(s, 3, 0)), zm),
            (yset(s, 3), yset(s, 0), yp),
            (yset(s, 1), yset(s, 0), ym),
            (wb.at[1, s, pl.ds(0, 4), yi[2]], wb.at[1, s, pl.ds(0, 4), yi[3]], yp),
            (wb.at[1, s, pl.ds(4, 4), yi[2]], wb.at[1, s, pl.ds(4, 4), yi[1]], ym),
        ]

    def send(core, s, m):
        _, src, dev = messages(core, s)[m]
        remote(src, src, g_send.at[s, m], g_recv.at[s, m], dev).start()

    def got(core, s, m):
        here, _, dev = messages(core, s)[m]
        remote(here, here, g_send.at[s, m], g_recv.at[s, m], dev).wait_recv()

    def sent(core, s, m):
        _, src, dev = messages(core, s)[m]
        remote(src, src, g_send.at[s, m], g_recv.at[s, m], dev).wait_send()

    def ring_stage(core, s, k):
        if k > 0:
            got(core, s, 2 * k - 2)
            got(core, s, 2 * k - 1)
        if k < 6:
            send(core, s, 2 * k)
            send(core, s, 2 * k + 1)
        else:
            half = wb.at[core, s]
            remote(half, half, sib_send.at[s], sib_recv.at[s], sib).start()

    def has(core, s):
        return (s != 1) if core == 0 else True

    def expander(g, rows, kind):
        i = lax.broadcasted_iota(jnp.int32, (rows, 256), 0)
        j = lax.broadcasted_iota(jnp.int32, (rows, 256), 1)
        return jnp.where((i & 127) == 4 * g + (j >> 6), 1.0, 0.0).astype(kind)

    def project(w):
        mixed = dot(tokv[...], w)
        v = valid[...]
        for half in range(2):
            part = mixed[:, half * 128 : half * 128 + 128] * v
            conv[half] = part.astype(BF16).astype(F32)

    def convolve(half, j, index):
        lanes = slice(half * 128, half * 128 + 128)
        acc = jnp.broadcast_to(cw_ref[index, 4:5, lanes], (CH, 128))
        for k in range(4):
            acc = acc + cw_ref[index, k : k + 1, lanes] * conv[half, pl.ds(13 + k + CH * j, CH), :]
        return (0.5 * acc * (1.0 + jnp.tanh(0.5 * acc))).astype(BF16)

    def halves(v):
        top = v.astype(BF16)
        low = (v - top.astype(F32)).astype(BF16)
        return top, low

    ri = lax.broadcasted_iota(jnp.int32, (CH, CH), 0)
    ci = lax.broadcasted_iota(jnp.int32, (CH, CH), 1)

    def prepare():
        raw = dot(tokv[pl.ds(HALO, SPAN), :], wb[1, 0].reshape(D, 128))
        project(jnp.concatenate([wb[0, 0].reshape(D, 128), wb[1, 1].reshape(D, 128)], axis=1))
        tri = jnp.where(ri >= ci, 1.0, 0.0)
        before = jnp.zeros((1, 128), F32)
        for j in range(NCH):
            rows = slice(j * CH, (j + 1) * CH)
            b = convolve(0, j, 0)
            cj = convolve(1, j, 0)
            cc[j] = jnp.concatenate([cj, cj], axis=1)
            bt[j] = b.astype(F32).T.astype(BF16)
            score = lax.dot_general(cj, b, (((1,), (1,)), ((), ())), preferred_element_type=F32)
            sc[j] = jnp.where(ri >= ci, score, 0.0)
            v = raw[rows] + hv_ref[0:1, :]
            step = jnp.maximum(v, 0.0) + jnp.log1p(jnp.exp(-jnp.abs(v)))
            step = step * valid[pl.ds(HALO + j * CH, CH), :]
            total = dot(tri, -step * hv_ref[1:2, :], precision=HIGH)
            cum[pl.ds(j * CH, CH), :] = total
            cum_t[j] = total.T
            step_t[j] = step.T
            end = total[CH - 1 : CH, :]
            top, low = halves(jnp.exp(end - total) * step)
            wk[pl.ds(j * CH, CH), :] = jnp.concatenate([top, low], axis=1)
            top, low = halves(jnp.exp(total))
            ec[pl.ds(j * CH, CH), :] = jnp.concatenate([top, low], axis=1)
            dc[j : j + 1, :] = jnp.exp(end)
            dc[4 + j : 5 + j, :] = jnp.exp(before)
            before = before + end
        ta[q] = jnp.broadcast_to(before, (8, 128))
        for d in range(1, 8):
            remote(ta.at[q], ta.at[q], t_send.at[d - 1], t_recv.at[d - 1], qn[d]).start()

    def link_decays():
        for d in range(1, 8):
            src = (q - d) % 8
            remote(ta.at[src], ta.at[src], t_send.at[d - 1], t_recv.at[d - 1], qn[d]).wait_recv()
        tot = [ta[d][0:1, :] for d in range(8)]
        dw[...] = jnp.zeros_like(dw)
        for xs in range(3):
            acc = jnp.zeros((1, 128), F32)
            for d in range(2 * xs + 2, 8):
                acc = acc + tot[d] * jnp.where(d < 2 * x, 1.0, 0.0)
            dw[xs : xs + 1, :] = jnp.exp(acc)
        dw[3:4, :] = jnp.exp(ta[2 * x][0:1, :])
        dw[4:5, :] = jnp.exp(ta[2 * x + 1][0:1, :])

    lane = lax.broadcasted_iota(jnp.int32, (CH, 128), 1)

    def group(g):
        s = g + 2
        project(jnp.concatenate([wb[0, s].reshape(D, 128), wb[1, s].reshape(D, 128)], axis=1))
        spread = expander(g, 256, BF16)
        decays = dot(dc[...], expander(g, 128, F32), precision=HIGH)
        cums = cum[...]
        for j in range(NCH):
            xj = [convolve(half, j, g + 1) for half in range(2)]
            weight = dot(wk[pl.ds(j * CH, CH), :], spread)
            xf = jnp.concatenate(xj, axis=1).astype(F32)
            local = dot(bt[j], (weight * xf).astype(BF16))
            if j > 0:
                local = local + decays[j : j + 1, :] * lb[g, j - 1]
            if j < NCH - 1:
                lb[g, j] = local
            else:
                dst[g] = local
            for half in range(2):
                mix = []
                for e in range(2):
                    h = 2 * half + e
                    cq = jnp.broadcast_to(cums[j * CH : (j + 1) * CH, h : h + 1], (CH, CH))
                    ck = cum_t[j, pl.ds(4 * g + h, 1), :]
                    sk = step_t[j, pl.ds(4 * g + h, 1), :]
                    mix.append((jnp.exp(jnp.minimum(cq - ck, 0.0)) * sc[j] * sk).astype(BF16))
                zero = jnp.zeros_like(xj[half])
                pair = jnp.concatenate(
                    [jnp.where(lane < 64, xj[half], zero), jnp.where(lane < 64, zero, xj[half])],
                    axis=0,
                )
                inner = dot(jnp.concatenate(mix, axis=1), pair)
                lanes = slice(half * 128, half * 128 + 128)
                skip = cw_ref[g + 1, 5:6, lanes]
                out[g, pl.ds(j * CH, CH), lanes] = inner + skip * xj[half].astype(F32)
        cum[...] = pltpu.roll(cums, 124, 1)

        @pl.when(c == 0)
        def _():
            remote(dst.at[g], d0.at[g], d_send.at[g], d_recv.at[g], sib).start()

    def chip_total(g):
        @pl.when(c == 1)
        def _():
            remote(dst.at[g], d0.at[g], d_send.at[g], d_recv.at[g], sib).wait_recv()
            decays = dot(dw[...], expander(g, 128, F32), precision=HIGH)
            tb[g] = (decays[4:5, :] * d0[g] + dst[g]).astype(BF16)
            for dx in range(1, 4):
                @pl.when(x + dx < 4)
                def _():
                    remote(
                        tb.at[g], tr.at[dx - 1, g], x_send.at[dx - 1, g], x_recv.at[dx - 1, g],
                        qn[2 * dx],
                    ).start()

    def chip_entry(g):
        @pl.when(c == 1)
        def _():
            decays = dot(dw[...], expander(g, 128, F32), precision=HIGH)
            ib[g] = jnp.zeros((128, 256), F32)
            for dx in range(1, 4):
                for xs in range(4 - dx):
                    @pl.when(x == xs + dx)
                    def _():
                        remote(
                            tb.at[g], tr.at[dx - 1, g], x_send.at[dx - 1, g],
                            x_recv.at[dx - 1, g], qn[2 * dx],
                        ).wait_recv()
                        ib[g] += decays[xs : xs + 1, :] * tr[dx - 1, g].astype(F32)
            remote(ib.at[g], ib.at[g], i_send.at[g], i_recv.at[g], sib).start()

    def late(g):
        spread = expander(g, 256, BF16)
        small = expander(g, 128, F32)
        inner = dot(dc[...], small, precision=HIGH)
        outer = dot(dw[...], small, precision=HIGH)

        @pl.when(c == 0)
        def _():
            remote(ib.at[g], ib.at[g], i_send.at[g], i_recv.at[g], sib).wait_recv()
            d0[g] = ib[g]

        @pl.when(c == 1)
        def _():
            d0[g] = d0[g] + outer[3:4, :] * ib[g]

        incoming = d0[g]
        for j in range(NCH):
            entry = inner[4 + j : 5 + j, :] * incoming
            if j > 0:
                entry = entry + lb[g, j - 1]
            carried = dot(cc[j], jnp.concatenate(halves(entry), axis=0))
            carried = carried * dot(ec[pl.ds(j * CH, CH), :], spread)
            full = out[g, pl.ds(j * CH, CH), :] + carried
            out[g, pl.ds(j * CH, CH), :] = full
            square = full * full
            ssq[pl.ds(j * CH, CH), :] += square[:, :128] + square[:, 128:]

        @pl.when(q == 7)
        def _():
            leaving = outer[4:5, :] * incoming + dst[g]
            fb[pl.ds(4 * g, 4)] = leaving.T.reshape(4, 64, 128).astype(BF16)
            for dest in range(7):
                @pl.when(g == DONE_AT[dest])
                def _():
                    remote(
                        fb.at[pl.ds(5 * dest, 5)], zg.at[z], f_send.at[dest], f_recv, (r, dest)
                    ).start()

    def body(t, carry):
        for k in range(7):
            s = t - k
            @pl.when((s >= 0) & (s < SLOTS))
            def _():
                @pl.when((c == 0) & has(0, s))
                def _():
                    ring_stage(0, s, k)

                @pl.when(c == 1)
                def _():
                    ring_stage(1, s, k)
        s = t - LAG
        @pl.when((s >= 0) & (s < SLOTS))
        def _():
            @pl.when(c == 0)
            def _():
                half = wb.at[1, s]
                remote(half, half, sib_send.at[s], sib_recv.at[s], sib).wait_recv()

            @pl.when((c == 1) & has(0, s))
            def _():
                half = wb.at[0, s]
                remote(half, half, sib_send.at[s], sib_recv.at[s], sib).wait_recv()

        g = s - 2

        @pl.when(g == -1)
        def _():
            prepare()

        @pl.when((g >= 0) & (g < GROUPS))
        def _():
            group(g)

        @pl.when(g == 0)
        def _():
            link_decays()

        @pl.when((g >= 1) & (g < GROUPS + 1))
        def _():
            chip_total(g - 1)

        @pl.when((g >= 2) & (g < GROUPS + 2))
        def _():
            chip_entry(g - 2)

        @pl.when((g >= 3) & (g < GROUPS + 3))
        def _():
            late(g - 3)

        return carry

    lax.fori_loop(0, LAG + SLOTS + 3, body, 0)

    def zroute(m):
        heads = [pl.ds(0, 5)] * 6 + [pl.ds(0, 3), pl.ds(3, 2)]
        dz = [0, 0, 7, 1, 6, 2, 5, 3][m]
        here = [7, 1, 6, 2, 5, 3, 4, 4][m]
        src = zg.at[zi[dz], heads[m]]
        to = zg.at[zi[here], heads[m]]
        dev = zp if m % 2 == 0 else zm
        return (
            remote(src, src, z_send.at[m], z_recv.at[m], dev),
            remote(to, to, z_send.at[m], z_recv.at[m], dev),
        )

    @pl.when(q == 7)
    def _():
        zg[z] = fb[35:40]

    @pl.when(q != 7)
    def _():
        remote(fb.at[pl.ds(0, 5)], zg.at[z], f_send.at[0], f_recv, (r, 0)).wait_recv()

    zroute(0)[0].start()
    zroute(1)[0].start()

    o_copies = []

    def normed(j):
        rows = pl.ds(j * CH, CH)
        mean = jnp.sum(ssq[rows, :], axis=1, keepdims=True) * (1.0 / D)
        factor = lax.rsqrt(mean + EPS) * valid[pl.ds(HALO + j * CH, CH), :][:, 0:1]
        for g in range(GROUPS):
            gain = cw_ref[g + 1, 6:7, :]
            resv[rows, 256 * g : 256 * g + 256] = (out[g, rows, :] * factor * gain).astype(BF16)
        copy = pltpu.make_async_copy(resv.at[rows], res_hbm.at[rows], o_sem.at[j])
        copy.start()
        o_copies.append(copy)

    for k in range(3):
        normed(k)
        for e in range(2):
            zroute(2 * k + e)[1].wait_recv()
            zroute(2 * k + 2 + e)[0].start()
    normed(3)
    for e in range(2):
        zroute(6 + e)[1].wait_recv()

    def holder(dy):
        target = z * 4 + yi[dy]

        def look(s, found):
            return jnp.where(deal_s[s] == target, s, found)

        return lax.fori_loop(0, 32, look, 0)

    y_copies = []
    for dy in range(1, 4):
        ys[dy - 1] = zg[holder(dy) // 4]
        copy = remote(ys.at[dy - 1], yr.at[dy], y_send.at[dy - 1], y_recv.at[dy - 1], yn[dy])
        copy.start()
        y_copies.append(copy)
    mine = holder(0)
    yr[0] = zg[mine // 4]
    for copy in y_copies:
        copy.wait_recv()
    fin_ref[...] = yr[(y + 4 - mine % 4) % 4].astype(F32)

    for copy in y_copies:
        copy.wait_send()
    for m in range(8):
        zroute(m)[0].wait_send()
    for copy in o_copies:
        copy.wait()
    for d in range(1, 8):
        remote(ta.at[q], ta.at[q], t_send.at[d - 1], t_recv.at[d - 1], qn[d]).wait_send()

    def drain_slot(s, carry):
        for core in range(2):
            @pl.when((c == core) & has(core, s))
            def _():
                for m in range(12):
                    sent(core, s, m)
                half = wb.at[core, s]
                remote(half, half, sib_send.at[s], sib_recv.at[s], sib).wait_send()
        return carry

    lax.fori_loop(0, SLOTS, drain_slot, 0)

    def drain_group(g, carry):
        @pl.when(c == 0)
        def _():
            remote(dst.at[g], d0.at[g], d_send.at[g], d_recv.at[g], sib).wait_send()

        @pl.when(c == 1)
        def _():
            remote(ib.at[g], ib.at[g], i_send.at[g], i_recv.at[g], sib).wait_send()
            for dx in range(1, 4):
                @pl.when(x + dx < 4)
                def _():
                    remote(
                        tb.at[g], tr.at[dx - 1, g], x_send.at[dx - 1, g], x_recv.at[dx - 1, g],
                        qn[2 * dx],
                    ).wait_send()
        return carry

    lax.fori_loop(0, GROUPS, drain_group, 0)

    @pl.when(q == 7)
    def _():
        for dest in range(7):
            remote(
                fb.at[pl.ds(5 * dest, 5)], zg.at[z], f_send.at[dest], f_recv, (r, dest)
            ).wait_send()


def on_device(
    tokens, mix_weight, step_weight, conv_weight, conv_bias, step_bias, decay_rate,
    skip_gain, norm_gain, prompt_len, prompt_start, deal,
):
    heads = decay_rate.shape[0]
    tiles = mix_weight.reshape(10, 22, 128)
    step_tile = jnp.pad(step_weight, ((0, 0), (0, 128 - heads)))[:, None]
    even = jnp.concatenate([tiles[:, 20:21], jnp.zeros_like(step_tile), tiles[:, 0:20:2]], axis=1)
    odd = jnp.concatenate([step_tile, tiles[:, 21:22], tiles[:, 1:20:2]], axis=1)
    wl = jnp.pad(jnp.stack([even, odd]).reshape(2, 10, 1536), ((0, 0), (0, 6), (0, 0)))
    per_head = 2560 // heads
    extra = jnp.stack([conv_bias[:2560], jnp.repeat(skip_gain, per_head), norm_gain,
                       jnp.zeros_like(norm_gain)])
    cw_x = jnp.concatenate([conv_weight[:, :2560], extra]).reshape(8, GROUPS, 256)
    cw_bc = jnp.pad(
        jnp.concatenate([conv_weight[:, 2560:], conv_bias[None, 2560:]]), ((0, 3), (0, 0))
    )
    cw = jnp.concatenate([cw_bc[:, None], cw_x], axis=1).transpose(1, 0, 2)
    hv = jnp.pad(jnp.stack([step_bias, decay_rate]), ((0, 6), (0, 128 - heads)))

    vm, dma = pltpu.VMEM, pltpu.SemaphoreType.DMA
    vspec = pl.BlockSpec(memory_space=pltpu.VMEM)
    sspec = pl.BlockSpec(memory_space=pltpu.SMEM)
    aspec = pl.BlockSpec(memory_space=pl.ANY)
    result, final = pl.pallas_call(
        kernel,
        out_shape=(
            jax.ShapeDtypeStruct((SPAN, D), BF16),
            jax.ShapeDtypeStruct((5, 64, 128), F32),
        ),
        in_specs=[aspec, vspec, vspec, vspec, sspec, sspec, sspec],
        out_specs=(aspec, vspec),
        scratch_shapes=[
            vm((2, SLOTS, 8, 4, 80, 128), BF16),
            vm((8, 16, 1536), BF16),
            vm((SPAN + HALO, D), BF16),
            vm((SPAN + HALO, 128), F32),
            vm((2, SPAN + HALO, 128), F32),
            vm((GROUPS, SPAN, 256), F32),
            vm((SPAN, D), BF16),
            vm((SPAN, 128), F32),
            vm((NCH, 128, CH), F32),
            vm((NCH, 128, CH), F32),
            vm((SPAN, 256), BF16),
            vm((SPAN, 256), BF16),
            vm((NCH, CH, CH), F32),
            vm((NCH, 128, CH), BF16),
            vm((NCH, CH, 256), BF16),
            vm((8, 128), F32),
            vm((8, 128), F32),
            vm((8, 8, 128), F32),
            vm((GROUPS, 3, 128, 256), F32),
            vm((GROUPS, 128, 256), F32),
            vm((GROUPS, 128, 256), F32),
            vm((GROUPS, 128, 256), BF16),
            vm((3, GROUPS, 128, 256), BF16),
            vm((GROUPS, 128, 256), F32),
            vm((40, 64, 128), BF16),
            vm((8, 5, 64, 128), BF16),
            vm((3, 5, 64, 128), BF16),
            vm((4, 5, 64, 128), BF16),
            vm((SPAN, 128), F32),
            dma((7,)), dma((8,)), dma((2,)), dma,
            dma((SLOTS, 12)), dma((SLOTS, 12)), dma((SLOTS,)), dma((SLOTS,)),
            dma((7,)), dma((7,)), dma((GROUPS,)), dma((GROUPS,)),
            dma((3, GROUPS)), dma((3, GROUPS)), dma((GROUPS,)), dma((GROUPS,)),
            dma((7,)), dma, dma((8,)), dma((8,)), dma((3,)), dma((3,)), dma((NCH,)),
        ],
        compiler_params=pltpu.CompilerParams(
            collective_id=0, has_side_effects=True, vmem_limit_bytes=62 * 1024 * 1024
        ),
    )(tokens[0], wl, cw, hv, prompt_len, prompt_start, deal)
    return (result[None], final[None])


def solution(mesh):
    return jax.shard_map(
        on_device,
        mesh=mesh,
        in_specs=(P("req", "seq", None), P(("req", "seq"), None), P(("req", "seq"), None))
        + (P(),) * 9,
        out_specs=(P("req", "seq", None), P("req", "seq", None, None)),
        check_vma=False,
    )
```

```python
import functools

import jax
import jax.numpy as jnp
from jax import lax
from jax.experimental import pallas as pl
from jax.experimental.pallas import tpu as pltpu
from jax.sharding import PartitionSpec as P

F32, BF16 = jnp.float32, jnp.bfloat16
MESH = pl.DeviceIdType.MESH
HIGH = lax.Precision.HIGHEST
EPS = 1e-05

SPAN = 512
HALO = 16
CH = 128
NCH = SPAN // CH
D = 2560
SLOTS = 12
GROUPS = 10
GAP = 2
LAG = 6 * GAP + 1
LOG2E = 1.4426950408889634
TO_TOTAL, TO_ENTRY, TO_LATE = 1, 3, 5


def dot(a, b, **kw):
    return jnp.dot(a, b, preferred_element_type=F32, **kw)


def kernel(
    tok_hbm, mix_ref, sw_ref, cw_ref, vec_ref, len_s, start_s, deal_s,
    res_hbm, fin_ref,
    wb, wl_ref, stage, tokv, valid, conv, hold, out, resv, cum, cum_t, wk, ec, sc, bt, cc,
    dcw, dx, ta, lb, dst, d0, tb, tr, ib, fd, zg, ys, yr, ssq,
    w_send, w_recv, h_sem, tok_sem, g_send, g_recv, sib_send, sib_recv,
    t_send, t_recv, d_send, d_recv, x_send, x_recv, i_send, i_recv,
    f_send, f_recv, z_send, z_recv, y_send, y_recv, o_sem,
):
    r, q = lax.axis_index("req"), lax.axis_index("seq")
    z, y, x, c = r // 4, r % 4, q // 2, q % 2
    yn = [(z * 4 + (y + d) % 4, q) for d in range(4)]
    zn = [(((z + d) % 8) * 4 + y, q) for d in range(8)]
    qn = [(r, (q + d) % 8) for d in range(8)]
    yp, ym, zp, zm = yn[1], yn[3], zn[1], zn[7]
    sib = (r, q + 1 - 2 * c)
    yi = [(y + d) % 4 for d in range(4)]
    zi = [(z + d) % 8 for d in range(8)]

    def remote(src, to, ssem, rsem, dev):
        return pltpu.make_async_remote_copy(
            src_ref=src, dst_ref=to, send_sem=ssem, recv_sem=rsem,
            device_id=dev, device_id_type=MESH,
        )

    barrier = pltpu.get_barrier_semaphore()
    partners = qn[1:] + yn[1:] + [zp, zm]
    for dev in partners:
        pl.semaphore_signal(barrier, inc=1, device_id=dev, device_id_type=MESH)
    tok_copy = pltpu.make_async_copy(tok_hbm, tokv.at[pl.ds(HALO, SPAN)], tok_sem)
    tok_copy.start()
    wl_ref[...] = jnp.zeros_like(wl_ref)
    wl_ref[0, 0:10, 0:40] = sw_ref[...]
    wl_ref[0, 0:10, 256:1536] = mix_ref[:, 0:1280]
    wl_ref[1, 0:10, 0:256] = mix_ref[:, 2560:2816]
    wl_ref[1, 0:10, 256:1536] = mix_ref[:, 1280:2560]
    pl.semaphore_wait(barrier, len(partners))

    waves = [pl.ds(0, 256), pl.ds(256, 1280)]
    w_copies = []
    for n, cols in enumerate(waves):
        own_w = pltpu.make_async_copy(wl_ref.at[c, :, cols], stage.at[q, :, cols], w_recv.at[n, 7])
        own_w.start()
        w_copies.append([own_w])
        for d in range(1, 8):
            to = (q + d) % 8
            copy = remote(
                wl_ref.at[to % 2, :, cols], stage.at[q, :, cols],
                w_send.at[n, d - 1], w_recv.at[n, d - 1], qn[d],
            )
            copy.start()
            w_copies[n].append(copy)
    halo = remote(
        tok_hbm.at[pl.ds(SPAN - HALO, HALO)], tokv.at[pl.ds(0, HALO)],
        h_sem.at[0], h_sem.at[1], qn[1],
    )
    halo.start()

    def holder(dy):
        target = z * 4 + yi[dy]

        def look(s, found):
            return jnp.where(deal_s[s] == target, s, found)

        return lax.fori_loop(0, 32, look, 0)

    for dy in range(4):
        hold[dy] = holder(dy)
    request = deal_s[r]
    first = start_s[request]
    last = first + len_s[request]
    place = lax.broadcasted_iota(jnp.int32, (SPAN + HALO, 128), 0) + (q * SPAN - HALO)
    valid[...] = jnp.where((place >= first) & (place < last), 1.0, 0.0)
    ssq[...] = jnp.zeros_like(ssq)

    row = lax.broadcasted_iota(jnp.int32, (80, 128), 0)
    col = lax.broadcasted_iota(jnp.int32, (80, 128), 1)
    pick = jnp.where(col == (row // 10) * 16 + row % 10, 1.0, 0.0).astype(BF16)

    def assemble(n, slots):
        w_copies[n][0].wait()
        for d in range(1, 8):
            to = stage.at[(q - d) % 8, :, waves[n]]
            remote(to, to, w_send.at[n, d - 1], w_recv.at[n, d - 1], qn[d]).wait_recv()
        for s in slots:
            part = stage[:, :, s * 128 : (s + 1) * 128].reshape(128, 128)
            wb[c, s, z, y] = dot(pick, part).astype(BF16)

    def blk(s, dz, dy):
        return wb.at[c, s, zi[dz], yi[dy]]

    def lo(ref):
        return ref.at[pl.ds(0, 48)]

    def hi(ref):
        return ref.at[pl.ds(48, 32)]

    def zset(s, dz):
        return wb.at[0, s, zi[dz]]

    def yset(s, dy):
        return wb.at[1, s, :, yi[dy]]

    def messages(core, s):
        if core == 0:
            return [
                (blk(s, 0, 3), blk(s, 0, 0), yp),
                (blk(s, 0, 1), blk(s, 0, 0), ym),
                (lo(blk(s, 0, 2)), lo(blk(s, 0, 3)), yp),
                (hi(blk(s, 0, 2)), hi(blk(s, 0, 1)), ym),
                (zset(s, 7), zset(s, 0), zp),
                (zset(s, 1), zset(s, 0), zm),
                (zset(s, 6), zset(s, 7), zp),
                (zset(s, 2), zset(s, 1), zm),
                (zset(s, 5), zset(s, 6), zp),
                (zset(s, 3), zset(s, 2), zm),
                (zset(s, 4).at[pl.ds(0, 2)], zset(s, 5).at[pl.ds(0, 2)], zp),
                (zset(s, 4).at[pl.ds(2, 2)], zset(s, 3).at[pl.ds(2, 2)], zm),
            ]
        return [
            (blk(s, 7, 0), blk(s, 0, 0), zp),
            (blk(s, 1, 0), blk(s, 0, 0), zm),
            (blk(s, 6, 0), blk(s, 7, 0), zp),
            (blk(s, 2, 0), blk(s, 1, 0), zm),
            (blk(s, 5, 0), blk(s, 6, 0), zp),
            (blk(s, 3, 0), blk(s, 2, 0), zm),
            (lo(blk(s, 4, 0)), lo(blk(s, 5, 0)), zp),
            (hi(blk(s, 4, 0)), hi(blk(s, 3, 0)), zm),
            (yset(s, 3), yset(s, 0), yp),
            (yset(s, 1), yset(s, 0), ym),
            (wb.at[1, s, pl.ds(0, 4), yi[2]], wb.at[1, s, pl.ds(0, 4), yi[3]], yp),
            (wb.at[1, s, pl.ds(4, 4), yi[2]], wb.at[1, s, pl.ds(4, 4), yi[1]], ym),
        ]

    def send(core, s, m):
        _, src, dev = messages(core, s)[m]
        remote(src, src, g_send.at[s, m], g_recv.at[s, m], dev).start()

    def got(core, s, m):
        here, _, dev = messages(core, s)[m]
        remote(here, here, g_send.at[s, m], g_recv.at[s, m], dev).wait_recv()

    def sent(core, s, m):
        _, src, dev = messages(core, s)[m]
        remote(src, src, g_send.at[s, m], g_recv.at[s, m], dev).wait_send()

    def ring_stage(core, s, k):
        if k > 0:
            got(core, s, 2 * k - 2)
            got(core, s, 2 * k - 1)
        if k < 6:
            send(core, s, 2 * k)
            send(core, s, 2 * k + 1)
        else:
            half = wb.at[core, s]
            remote(half, half, sib_send.at[s], sib_recv.at[s], sib).start()

    def has(core, s):
        return (s != 1) if core == 0 else True

    def expander(g, rows, kind):
        i = lax.broadcasted_iota(jnp.int32, (rows, 256), 0)
        j = lax.broadcasted_iota(jnp.int32, (rows, 256), 1)
        head = 2 * g + 20 * (j >> 7) + ((j >> 6) & 1)
        return jnp.where((i & 127) == head, 1.0, 0.0).astype(kind)

    def project(w):
        mixed = dot(tokv[...], w)
        v = valid[...]
        for half in range(2):
            part = mixed[:, half * 128 : half * 128 + 128] * v
            conv[half] = part.astype(BF16).astype(F32)

    def convolve(half, j, tile):
        lanes = pl.ds(pl.multiple_of(tile * 128, 128), 128)
        acc = jnp.broadcast_to(vec_ref[pl.ds(tile, 1), :], (CH, 128))
        for k in range(4):
            acc = acc + cw_ref[k : k + 1, lanes] * conv[half, pl.ds(13 + k + CH * j, CH), :]
        acc = 0.5 * acc
        return (acc + acc * jnp.tanh(acc)).astype(BF16)

    def halves(v):
        top = v.astype(BF16)
        low = (v - top.astype(F32)).astype(BF16)
        return top, low

    ri = lax.broadcasted_iota(jnp.int32, (CH, CH), 0)
    ci = lax.broadcasted_iota(jnp.int32, (CH, CH), 1)

    def prepare():
        tok_copy.wait()
        halo.wait_send()
        halo.wait_recv()
        raw = dot(tokv[pl.ds(HALO, SPAN), :], wb[0, 0].reshape(D, 128))
        project(jnp.concatenate([wb[1, 0].reshape(D, 128), wb[1, 1].reshape(D, 128)], axis=1))
        tri = jnp.where(ri >= ci, 1.0, 0.0)
        before = jnp.zeros((1, 128), F32)
        for j in range(NCH):
            rows = slice(j * CH, (j + 1) * CH)
            b = convolve(0, j, 20)
            cj = convolve(1, j, 21)
            cc[j] = jnp.concatenate([cj, cj], axis=1)
            bt[j] = b.astype(F32).T.astype(BF16)
            score = lax.dot_general(cj, b, (((1,), (1,)), ((), ())), preferred_element_type=F32)
            sc[j] = jnp.where(ri >= ci, score, 0.0)
            v = raw[rows] + vec_ref[42:43, :]
            step = jnp.maximum(v, 0.0) + jnp.log1p(jnp.exp(-jnp.abs(v)))
            step = step * valid[pl.ds(HALO + j * CH, CH), :]
            total = dot(tri, -step * vec_ref[43:44, :], precision=HIGH)
            cum[pl.ds(j * CH, CH), :] = total * LOG2E
            cum_t[j] = ((total - jnp.log(step)) * LOG2E).T
            end = total[CH - 1 : CH, :]
            top, low = halves(jnp.exp(end - total) * step)
            wk[pl.ds(j * CH, CH), :] = jnp.concatenate([top, low], axis=1)
            top, low = halves(jnp.exp(total))
            ec[pl.ds(j * CH, CH), :] = jnp.concatenate([top, low], axis=1)
            dcw[j : j + 1, :] = jnp.exp(end)
            dcw[4 + j : 5 + j, :] = jnp.exp(before)
            before = before + end
        dcw[8:9, :] = vec_ref[44:45, :]
        ta[q] = jnp.broadcast_to(before, (8, 128))
        for d in range(1, 8):
            remote(ta.at[q], ta.at[q], t_send.at[d - 1], t_recv.at[d - 1], qn[d]).start()

    def link_decays():
        for d in range(1, 8):
            src = (q - d) % 8
            remote(ta.at[src], ta.at[src], t_send.at[d - 1], t_recv.at[d - 1], qn[d]).wait_recv()
        tot = [ta[d][0:1, :] for d in range(8)]
        dcw[16:24, :] = jnp.zeros((8, 128), F32)
        def between(lower, upper):
            acc = jnp.zeros((1, 128), F32)
            for d in range(8):
                acc = acc + tot[d] * jnp.where((d >= lower) & (d < upper), 1.0, 0.0)
            return jnp.exp(acc)

        for m in range(1, 4):
            xs = (x - m) % 4
            dcw[15 + m : 16 + m, :] = between(2 * xs + 2, 2 * x) * jnp.where(xs < x, 1.0, 0.0)
            dcw[20 + m : 21 + m, :] = between(2 * xs + 2, 8)
        dcw[9:10, :] = between(2 * x + 2, 8)
        dcw[19:20, :] = jnp.exp(ta[2 * x][0:1, :])
        dcw[20:21, :] = jnp.exp(ta[2 * x + 1][0:1, :])

    lane = lax.broadcasted_iota(jnp.int32, (CH, 128), 1)

    def group(g):
        s = g + 2
        project(jnp.concatenate([wb[0, s].reshape(D, 128), wb[1, s].reshape(D, 128)], axis=1))
        spread = expander(g, 256, BF16)
        decays = dot(dcw[...], expander(g, 128, F32), precision=HIGH)
        dx[g] = decays
        cums = cum[...]
        for j in range(NCH):
            xj = [convolve(half, j, g + 10 * half) for half in range(2)]
            weight = dot(wk[pl.ds(j * CH, CH), :], spread)
            xf = jnp.concatenate(xj, axis=1).astype(F32)
            local = dot(bt[j], (weight * xf).astype(BF16))
            if j > 0:
                local = local + decays[j : j + 1, :] * lb[g, j - 1]
            if j < NCH - 1:
                lb[g, j] = local
            else:
                dst[g] = local
            for half in range(2):
                mix = []
                for e in range(2):
                    h = 20 * half + e
                    cq = jnp.broadcast_to(cums[j * CH : (j + 1) * CH, h : h + 1], (CH, CH))
                    ck = cum_t[j, pl.ds(2 * g + h, 1), :]
                    mix.append((jnp.exp2(jnp.minimum(cq - ck, 100.0)) * sc[j]).astype(BF16))
                zero = jnp.zeros_like(xj[half])
                pair = jnp.concatenate(
                    [jnp.where(lane < 64, xj[half], zero), jnp.where(lane < 64, zero, xj[half])],
                    axis=0,
                )
                inner = dot(jnp.concatenate(mix, axis=1), pair)
                lanes = slice(half * 128, half * 128 + 128)
                skip = decays[8:9, lanes]
                out[g, pl.ds(j * CH, CH), lanes] = inner + skip * xj[half].astype(F32)
        cum[...] = pltpu.roll(cums, 126, 1)

        @pl.when(c == 0)
        def _():
            remote(dst.at[g], d0.at[g], d_send.at[g], d_recv.at[g], sib).start()

    def total_copy(g, m):
        return remote(
            tb.at[g], tr.at[m - 1, g], x_send.at[m - 1, g], x_recv.at[m - 1, g], qn[2 * m]
        )

    def chip_total(g):
        @pl.when(c == 1)
        def _():
            remote(dst.at[g], d0.at[g], d_send.at[g], d_recv.at[g], sib).wait_recv()
            tb[g] = (dx[g, 20:21, :] * d0[g] + dst[g]).astype(BF16)
            for m in range(1, 4):
                total_copy(g, m).start()

    def own_state():
        return remote(fd.at[0], zg.at[z], f_send, f_recv, sib)

    def chip_entry(g):
        @pl.when(c == 1)
        def _():
            for m in range(1, 4):
                total_copy(g, m).wait_recv()
            parts = [tr[m, g].astype(F32) for m in range(3)]
            entry = dx[g, 16:17, :] * parts[0] + dx[g, 17:18, :] * parts[1]
            ib[g] = entry + dx[g, 18:19, :] * parts[2]
            remote(ib.at[g], ib.at[g], i_send.at[g], i_recv.at[g], sib).start()
            for half in range(2):
                head = 20 * half + 2 * g
                lanes = slice(half * 128, half * 128 + 128)
                chips = [(head + e) // 10 for e in range(2)]

                @pl.when((chips[0] == x) | (chips[1] == x))
                def _():
                    leaving = dx[g, 9:10, lanes] * tb[g, :, lanes].astype(F32)
                    for m in range(3):
                        leaving += dx[g, 21 + m : 22 + m, lanes] * tr[m, g, :, lanes].astype(F32)
                    turned = leaving.T.reshape(2, 64, 128).astype(BF16)
                    for e in range(2):
                        @pl.when(chips[e] == x)
                        def _():
                            fd[((head + e) // 5) % 2, (head + e) % 5] = turned[e]

            @pl.when(g == 2 + 5 * (x % 2))
            def _():
                own_state().start()

            @pl.when(g == 4 + 5 * (x % 2))
            def _():
                zg[z] = fd[1]

    def late(g):
        spread = expander(g, 256, BF16)

        @pl.when(c == 0)
        def _():
            remote(ib.at[g], ib.at[g], i_send.at[g], i_recv.at[g], sib).wait_recv()
            d0[g] = ib[g]

        @pl.when(c == 1)
        def _():
            d0[g] = d0[g] + dx[g, 19:20, :] * ib[g]

        incoming = d0[g]
        for j in range(NCH):
            entry = dx[g, 4 + j : 5 + j, :] * incoming
            if j > 0:
                entry = entry + lb[g, j - 1]
            carried = dot(cc[j], jnp.concatenate(halves(entry), axis=0))
            carried = carried * dot(ec[pl.ds(j * CH, CH), :], spread)
            full = out[g, pl.ds(j * CH, CH), :] + carried
            out[g, pl.ds(j * CH, CH), :] = full
            square = full * full
            ssq[pl.ds(j * CH, CH), :] += square[:, :128] + square[:, 128:]

    def zroute(m, here):
        heads = [pl.ds(0, 5)] * 6 + [pl.ds(0, 3), pl.ds(3, 2)]
        dz = ([7, 1, 6, 2, 5, 3, 4, 4] if here else [0, 0, 7, 1, 6, 2, 5, 3])[m]
        ref = zg.at[zi[dz], heads[m]]
        return remote(ref, ref, z_send.at[m], z_recv.at[m], zp if m % 2 == 0 else zm)

    def y_copy(dy):
        return remote(ys.at[dy - 1], yr.at[dy], y_send.at[dy - 1], y_recv.at[dy - 1], yn[dy])

    def route(k):
        if k == 0:
            @pl.when(c == 0)
            def _():
                own_state().wait_recv()
        elif k < 5:
            zroute(2 * k - 2, True).wait_recv()
            zroute(2 * k - 1, True).wait_recv()
        if k < 4:
            zroute(2 * k, False).start()
            zroute(2 * k + 1, False).start()
        elif k == 4:
            for dy in range(1, 4):
                ys[dy - 1] = zg[hold[dy] // 4]
                y_copy(dy).start()
            yr[0] = zg[hold[0] // 4]
        else:
            for dy in range(1, 4):
                y_copy(dy).wait_recv()
            fin_ref[...] = yr[(y + 4 - hold[0] % 4) % 4].astype(F32)

    def normed(j):
        rows = pl.ds(j * CH, CH)
        mean = jnp.sum(ssq[rows, :], axis=1, keepdims=True) * (1.0 / D)
        factor = lax.rsqrt(mean + EPS) * valid[pl.ds(HALO + j * CH, CH), :][:, 0:1]
        for g in range(GROUPS):
            for half in range(2):
                tile = g + 10 * half
                gain = vec_ref[22 + tile : 23 + tile, :]
                part = out[g, rows, 128 * half : 128 * half + 128] * factor * gain
                resv[rows, 128 * tile : 128 * tile + 128] = part.astype(BF16)
        out_copy(j).start()

    def out_copy(j):
        rows = pl.ds(j * CH, CH)
        return pltpu.make_async_copy(resv.at[rows], res_hbm.at[rows], o_sem.at[j])

    def body(t, carry):
        for k in range(7):
            s = t - GAP * k
            @pl.when((s >= (0 if k else 2)) & (s < SLOTS))
            def _():
                @pl.when((c == 0) & has(0, s))
                def _():
                    ring_stage(0, s, k)

                @pl.when(c == 1)
                def _():
                    ring_stage(1, s, k)
        s = t - LAG
        @pl.when((s >= 0) & (s < SLOTS))
        def _():
            @pl.when(c == 0)
            def _():
                half = wb.at[1, s]
                remote(half, half, sib_send.at[s], sib_recv.at[s], sib).wait_recv()

            @pl.when((c == 1) & has(0, s))
            def _():
                half = wb.at[0, s]
                remote(half, half, sib_send.at[s], sib_recv.at[s], sib).wait_recv()

        g = s - 2

        @pl.when(g == -1)
        def _():
            prepare()

        @pl.when(g == 0)
        def _():
            link_decays()

        @pl.when((g >= 0) & (g < GROUPS))
        def _():
            group(g)

        @pl.when((g >= TO_TOTAL) & (g < GROUPS + TO_TOTAL))
        def _():
            chip_total(g - TO_TOTAL)

        @pl.when((g >= TO_ENTRY) & (g < GROUPS + TO_ENTRY))
        def _():
            chip_entry(g - TO_ENTRY)

        for k in range(6):
            @pl.when(g == TO_ENTRY + 3 + 2 * c + 5 * (x % 2) + k)
            def _():
                route(k)

        @pl.when((g >= TO_LATE) & (g < GROUPS + TO_LATE))
        def _():
            late(g - TO_LATE)

        for j in range(NCH):
            @pl.when(g == GROUPS + TO_LATE + j)
            def _():
                normed(j)

        return carry

    assemble(0, range(2))
    for s in range(2):
        for core in range(2):
            if core == 1 or s != 1:
                @pl.when(c == core)
                def _():
                    ring_stage(core, s, 0)
    assemble(1, range(2, SLOTS))
    lax.fori_loop(0, LAG + 2 + GROUPS + TO_LATE + 4, body, 0)

    for copies in w_copies:
        for copy in copies[1:]:
            copy.wait_send()
    for dy in range(1, 4):
        y_copy(dy).wait_send()
    for m in range(8):
        zroute(m, False).wait_send()
    for j in range(NCH):
        out_copy(j).wait()
    for d in range(1, 8):
        remote(ta.at[q], ta.at[q], t_send.at[d - 1], t_recv.at[d - 1], qn[d]).wait_send()

    def drain_slot(s, carry):
        for core in range(2):
            @pl.when((c == core) & has(core, s))
            def _():
                for m in range(12):
                    sent(core, s, m)
                half = wb.at[core, s]
                remote(half, half, sib_send.at[s], sib_recv.at[s], sib).wait_send()
        return carry

    lax.fori_loop(0, SLOTS, drain_slot, 0)

    def drain_group(g, carry):
        @pl.when(c == 0)
        def _():
            remote(dst.at[g], d0.at[g], d_send.at[g], d_recv.at[g], sib).wait_send()

        @pl.when(c == 1)
        def _():
            remote(ib.at[g], ib.at[g], i_send.at[g], i_recv.at[g], sib).wait_send()
            for m in range(1, 4):
                total_copy(g, m).wait_send()
        return carry

    lax.fori_loop(0, GROUPS, drain_group, 0)

    @pl.when(c == 1)
    def _():
        own_state().wait_send()


def on_device(
    tokens, mix_weight, step_weight, conv_weight, conv_bias, step_bias, decay_rate,
    skip_gain, norm_gain, prompt_len, prompt_start, deal,
):
    heads = decay_rate.shape[0]
    gap = jnp.zeros((128 - heads,), F32)
    vec = jnp.concatenate(
        [conv_bias, norm_gain, step_bias, gap, decay_rate, gap, skip_gain, gap, jnp.zeros((384,), F32)]
    ).reshape(48, 128)

    vm, dma = pltpu.VMEM, pltpu.SemaphoreType.DMA
    vspec = pl.BlockSpec(memory_space=pltpu.VMEM)
    sspec = pl.BlockSpec(memory_space=pltpu.SMEM)
    aspec = pl.BlockSpec(memory_space=pl.ANY)
    result, final = pl.pallas_call(
        kernel,
        out_shape=(
            jax.ShapeDtypeStruct((SPAN, D), BF16),
            jax.ShapeDtypeStruct((5, 64, 128), F32),
        ),
        in_specs=[aspec, vspec, vspec, vspec, vspec, sspec, sspec, sspec],
        out_specs=(aspec, vspec),
        scratch_shapes=[
            vm((2, SLOTS, 8, 4, 80, 128), BF16),
            vm((2, 16, 1536), BF16),
            vm((8, 16, 1536), BF16),
            vm((SPAN + HALO, D), BF16),
            vm((SPAN + HALO, 128), F32),
            vm((2, SPAN + HALO, 128), F32),
            pltpu.SMEM((4,), jnp.int32),
            vm((GROUPS, SPAN, 256), F32),
            vm((SPAN, D), BF16),
            vm((SPAN, 128), F32),
            vm((NCH, 128, CH), F32),
            vm((SPAN, 256), BF16),
            vm((SPAN, 256), BF16),
            vm((NCH, CH, CH), F32),
            vm((NCH, 128, CH), BF16),
            vm((NCH, CH, 256), BF16),
            vm((24, 128), F32),
            vm((GROUPS, 24, 256), F32),
            vm((8, 8, 128), F32),
            vm((GROUPS, 3, 128, 256), F32),
            vm((GROUPS, 128, 256), F32),
            vm((GROUPS, 128, 256), F32),
            vm((GROUPS, 128, 256), BF16),
            vm((3, GROUPS, 128, 256), BF16),
            vm((GROUPS, 128, 256), F32),
            vm((2, 5, 64, 128), BF16),
            vm((8, 5, 64, 128), BF16),
            vm((3, 5, 64, 128), BF16),
            vm((4, 5, 64, 128), BF16),
            vm((SPAN, 128), F32),
            dma((2, 7)), dma((2, 8)), dma((2,)), dma,
            dma((SLOTS, 12)), dma((SLOTS, 12)), dma((SLOTS,)), dma((SLOTS,)),
            dma((7,)), dma((7,)), dma((GROUPS,)), dma((GROUPS,)),
            dma((3, GROUPS)), dma((3, GROUPS)), dma((GROUPS,)), dma((GROUPS,)),
            dma, dma, dma((8,)), dma((8,)), dma((3,)), dma((3,)), dma((NCH,)),
        ],
        compiler_params=pltpu.CompilerParams(
            collective_id=0, has_side_effects=True, vmem_limit_bytes=62 * 1024 * 1024
        ),
    )(tokens[0], mix_weight, step_weight, conv_weight, vec, prompt_len, prompt_start, deal)
    return (result[None], final[None])


def solution(mesh):
    return jax.shard_map(
        on_device,
        mesh=mesh,
        in_specs=(P("req", "seq", None), P(("req", "seq"), None), P(("req", "seq"), None))
        + (P(),) * 9,
        out_specs=(P("req", "seq", None), P("req", "seq", None, None)),
        check_vma=False,
    )
```

```python
import functools

import jax
import jax.numpy as jnp
from jax import lax
from jax.experimental import pallas as pl
from jax.experimental.pallas import tpu as pltpu
from jax.sharding import PartitionSpec as P

F32, BF16 = jnp.float32, jnp.bfloat16
MESH = pl.DeviceIdType.MESH
HIGH = lax.Precision.HIGHEST
EPS = 1e-05

SPAN = 512
HALO = 16
CH = 128
NCH = SPAN // CH
D = 2560
SLOTS = 12
GROUPS = 10
GAP = 2
LAG = 6 * GAP + 1
LOG2E = 1.4426950408889634
TO_TOTAL, TO_ENTRY, TO_LATE = 1, 3, 5


def dot(a, b, **kw):
    return jnp.dot(a, b, preferred_element_type=F32, **kw)


def kernel(
    tok_hbm, mix_ref, sw_ref, cw_ref, vec_ref, len_s, start_s, deal_s,
    res_ref, fin_ref,
    wb, wl_ref, stage, tokv, valid, conv, hold, out, cum, cum_t, wk, ec, sc, bt, cc,
    dcw, dx, ta, lb, dst, d0, tb, tr, ib, fd, zg, ys, yr, ssq,
    w_send, w_recv, h_sem, tok_sem, g_send, g_recv, sib_send, sib_recv,
    t_send, t_recv, d_send, d_recv, x_send, x_recv, i_send, i_recv,
    f_send, f_recv, z_send, z_recv, y_send, y_recv,
):
    r, q = lax.axis_index("req"), lax.axis_index("seq")
    z, y, x, c = r // 4, r % 4, q // 2, q % 2
    yn = [(z * 4 + (y + d) % 4, q) for d in range(4)]
    zn = [(((z + d) % 8) * 4 + y, q) for d in range(8)]
    qn = [(r, (q + d) % 8) for d in range(8)]
    yp, ym, zp, zm = yn[1], yn[3], zn[1], zn[7]
    sib = (r, q + 1 - 2 * c)
    yi = [(y + d) % 4 for d in range(4)]
    zi = [(z + d) % 8 for d in range(8)]

    def remote(src, to, ssem, rsem, dev):
        return pltpu.make_async_remote_copy(
            src_ref=src, dst_ref=to, send_sem=ssem, recv_sem=rsem,
            device_id=dev, device_id_type=MESH,
        )

    barrier = pltpu.get_barrier_semaphore()
    partners = qn[1:] + yn[1:] + [zp, zm]
    for dev in partners:
        pl.semaphore_signal(barrier, inc=1, device_id=dev, device_id_type=MESH)
    tok_copy = pltpu.make_async_copy(tok_hbm, tokv.at[pl.ds(HALO, SPAN)], tok_sem)
    tok_copy.start()
    wl_ref[...] = jnp.zeros_like(wl_ref)
    wl_ref[0, 0:10, 0:40] = sw_ref[...]
    wl_ref[0, 0:10, 256:1536] = mix_ref[:, 0:1280]
    wl_ref[1, 0:10, 0:256] = mix_ref[:, 2560:2816]
    wl_ref[1, 0:10, 256:1536] = mix_ref[:, 1280:2560]
    pl.semaphore_wait(barrier, len(partners))

    waves = [pl.ds(0, 256), pl.ds(256, 1280)]
    w_copies = []
    for n, cols in enumerate(waves):
        own_w = pltpu.make_async_copy(wl_ref.at[c, :, cols], stage.at[q, :, cols], w_recv.at[n, 7])
        own_w.start()
        w_copies.append([own_w])
        for d in range(1, 8):
            to = (q + d) % 8
            copy = remote(
                wl_ref.at[to % 2, :, cols], stage.at[q, :, cols],
                w_send.at[n, d - 1], w_recv.at[n, d - 1], qn[d],
            )
            copy.start()
            w_copies[n].append(copy)
    halo = remote(
        tok_hbm.at[pl.ds(SPAN - HALO, HALO)], tokv.at[pl.ds(0, HALO)],
        h_sem.at[0], h_sem.at[1], qn[1],
    )
    halo.start()

    def holder(dy):
        target = z * 4 + yi[dy]

        def look(s, found):
            return jnp.where(deal_s[s] == target, s, found)

        return lax.fori_loop(0, 32, look, 0)

    for dy in range(4):
        hold[dy] = holder(dy)
    request = deal_s[r]
    first = start_s[request]
    last = first + len_s[request]
    place = lax.broadcasted_iota(jnp.int32, (SPAN + HALO, 128), 0) + (q * SPAN - HALO)
    valid[...] = jnp.where((place >= first) & (place < last), 1.0, 0.0)
    ssq[...] = jnp.zeros_like(ssq)

    row = lax.broadcasted_iota(jnp.int32, (80, 128), 0)
    col = lax.broadcasted_iota(jnp.int32, (80, 128), 1)
    pick = jnp.where(col == (row // 10) * 16 + row % 10, 1.0, 0.0).astype(BF16)

    def assemble(n, slots):
        w_copies[n][0].wait()
        for d in range(1, 8):
            to = stage.at[(q - d) % 8, :, waves[n]]
            remote(to, to, w_send.at[n, d - 1], w_recv.at[n, d - 1], qn[d]).wait_recv()
        for s in slots:
            part = stage[:, :, s * 128 : (s + 1) * 128].reshape(128, 128)
            wb[c, s, z, y] = dot(pick, part).astype(BF16)

    def blk(s, dz, dy):
        return wb.at[c, s, zi[dz], yi[dy]]

    def lo(ref):
        return ref.at[pl.ds(0, 48)]

    def hi(ref):
        return ref.at[pl.ds(48, 32)]

    def zset(s, dz):
        return wb.at[0, s, zi[dz]]

    def yset(s, dy):
        return wb.at[1, s, :, yi[dy]]

    def messages(core, s):
        if core == 0:
            return [
                (blk(s, 0, 3), blk(s, 0, 0), yp),
                (blk(s, 0, 1), blk(s, 0, 0), ym),
                (lo(blk(s, 0, 2)), lo(blk(s, 0, 3)), yp),
                (hi(blk(s, 0, 2)), hi(blk(s, 0, 1)), ym),
                (zset(s, 7), zset(s, 0), zp),
                (zset(s, 1), zset(s, 0), zm),
                (zset(s, 6), zset(s, 7), zp),
                (zset(s, 2), zset(s, 1), zm),
                (zset(s, 5), zset(s, 6), zp),
                (zset(s, 3), zset(s, 2), zm),
                (zset(s, 4).at[pl.ds(0, 2)], zset(s, 5).at[pl.ds(0, 2)], zp),
                (zset(s, 4).at[pl.ds(2, 2)], zset(s, 3).at[pl.ds(2, 2)], zm),
            ]
        return [
            (blk(s, 7, 0), blk(s, 0, 0), zp),
            (blk(s, 1, 0), blk(s, 0, 0), zm),
            (blk(s, 6, 0), blk(s, 7, 0), zp),
            (blk(s, 2, 0), blk(s, 1, 0), zm),
            (blk(s, 5, 0), blk(s, 6, 0), zp),
            (blk(s, 3, 0), blk(s, 2, 0), zm),
            (lo(blk(s, 4, 0)), lo(blk(s, 5, 0)), zp),
            (hi(blk(s, 4, 0)), hi(blk(s, 3, 0)), zm),
            (yset(s, 3), yset(s, 0), yp),
            (yset(s, 1), yset(s, 0), ym),
            (wb.at[1, s, pl.ds(0, 4), yi[2]], wb.at[1, s, pl.ds(0, 4), yi[3]], yp),
            (wb.at[1, s, pl.ds(4, 4), yi[2]], wb.at[1, s, pl.ds(4, 4), yi[1]], ym),
        ]

    def send(core, s, m):
        _, src, dev = messages(core, s)[m]
        remote(src, src, g_send.at[s, m], g_recv.at[s, m], dev).start()

    def got(core, s, m):
        here, _, dev = messages(core, s)[m]
        remote(here, here, g_send.at[s, m], g_recv.at[s, m], dev).wait_recv()

    def sent(core, s, m):
        _, src, dev = messages(core, s)[m]
        remote(src, src, g_send.at[s, m], g_recv.at[s, m], dev).wait_send()

    def ring_stage(core, s, k):
        if k > 0:
            got(core, s, 2 * k - 2)
            got(core, s, 2 * k - 1)
        if k < 6:
            send(core, s, 2 * k)
            send(core, s, 2 * k + 1)
        else:
            half = wb.at[core, s]
            remote(half, half, sib_send.at[s], sib_recv.at[s], sib).start()

    def has(core, s):
        return (s != 1) if core == 0 else True

    def expander(g, rows, kind):
        i = lax.broadcasted_iota(jnp.int32, (rows, 256), 0)
        j = lax.broadcasted_iota(jnp.int32, (rows, 256), 1)
        head = 2 * g + 20 * (j >> 7) + ((j >> 6) & 1)
        return jnp.where((i & 127) == head, 1.0, 0.0).astype(kind)

    def project(w):
        mixed = dot(tokv[...], w)
        v = valid[...]
        for half in range(2):
            part = mixed[:, half * 128 : half * 128 + 128] * v
            conv[half] = part.astype(BF16).astype(F32)

    def convolve(half, j, tile):
        lanes = pl.ds(pl.multiple_of(tile * 128, 128), 128)
        acc = jnp.broadcast_to(vec_ref[pl.ds(tile, 1), :], (CH, 128))
        for k in range(4):
            acc = acc + cw_ref[k : k + 1, lanes] * conv[half, pl.ds(13 + k + CH * j, CH), :]
        acc = 0.5 * acc
        return (acc + acc * jnp.tanh(acc)).astype(BF16)

    def halves(v):
        top = v.astype(BF16)
        low = (v - top.astype(F32)).astype(BF16)
        return top, low

    ri = lax.broadcasted_iota(jnp.int32, (CH, CH), 0)
    ci = lax.broadcasted_iota(jnp.int32, (CH, CH), 1)

    def prepare():
        tok_copy.wait()
        halo.wait_send()
        halo.wait_recv()
        raw = dot(tokv[pl.ds(HALO, SPAN), :], wb[0, 0].reshape(D, 128))
        project(jnp.concatenate([wb[1, 0].reshape(D, 128), wb[1, 1].reshape(D, 128)], axis=1))
        tri = jnp.where(ri >= ci, 1.0, 0.0)
        before = jnp.zeros((1, 128), F32)
        for j in range(NCH):
            rows = slice(j * CH, (j + 1) * CH)
            b = convolve(0, j, 20)
            cj = convolve(1, j, 21)
            cc[j] = jnp.concatenate([cj, cj], axis=1)
            bt[j] = b.astype(F32).T.astype(BF16)
            score = lax.dot_general(cj, b, (((1,), (1,)), ((), ())), preferred_element_type=F32)
            sc[j] = jnp.where(ri >= ci, score, 0.0)
            v = raw[rows] + vec_ref[42:43, :]
            step = jnp.maximum(v, 0.0) + jnp.log1p(jnp.exp(-jnp.abs(v)))
            step = step * valid[pl.ds(HALO + j * CH, CH), :]
            total = dot(tri, -step * vec_ref[43:44, :], precision=HIGH)
            cum[pl.ds(j * CH, CH), :] = total * LOG2E
            cum_t[j] = ((total - jnp.log(step)) * LOG2E).T
            end = total[CH - 1 : CH, :]
            top, low = halves(jnp.exp(end - total) * step)
            wk[pl.ds(j * CH, CH), :] = jnp.concatenate([top, low], axis=1)
            top, low = halves(jnp.exp(total))
            ec[pl.ds(j * CH, CH), :] = jnp.concatenate([top, low], axis=1)
            dcw[j : j + 1, :] = jnp.exp(end)
            dcw[4 + j : 5 + j, :] = jnp.exp(before)
            before = before + end
        dcw[8:9, :] = vec_ref[44:45, :]
        ta[q] = jnp.broadcast_to(before, (8, 128))
        for d in range(1, 8):
            remote(ta.at[q], ta.at[q], t_send.at[d - 1], t_recv.at[d - 1], qn[d]).start()

    def link_decays():
        for d in range(1, 8):
            src = (q - d) % 8
            remote(ta.at[src], ta.at[src], t_send.at[d - 1], t_recv.at[d - 1], qn[d]).wait_recv()
        tot = [ta[d][0:1, :] for d in range(8)]
        dcw[16:24, :] = jnp.zeros((8, 128), F32)
        def between(lower, upper):
            acc = jnp.zeros((1, 128), F32)
            for d in range(8):
                acc = acc + tot[d] * jnp.where((d >= lower) & (d < upper), 1.0, 0.0)
            return jnp.exp(acc)

        for m in range(1, 4):
            xs = (x - m) % 4
            dcw[15 + m : 16 + m, :] = between(2 * xs + 2, 2 * x) * jnp.where(xs < x, 1.0, 0.0)
            dcw[20 + m : 21 + m, :] = between(2 * xs + 2, 8)
        dcw[9:10, :] = between(2 * x + 2, 8)
        dcw[19:20, :] = jnp.exp(ta[2 * x][0:1, :])
        dcw[20:21, :] = jnp.exp(ta[2 * x + 1][0:1, :])

    lane = lax.broadcasted_iota(jnp.int32, (CH, 128), 1)

    def group(g):
        s = g + 2
        project(jnp.concatenate([wb[0, s].reshape(D, 128), wb[1, s].reshape(D, 128)], axis=1))
        spread = expander(g, 256, BF16)
        decays = dot(dcw[...], expander(g, 128, F32), precision=HIGH)
        dx[g] = decays
        cums = cum[...]
        for j in range(NCH):
            xj = [convolve(half, j, g + 10 * half) for half in range(2)]
            weight = dot(wk[pl.ds(j * CH, CH), :], spread)
            xf = jnp.concatenate(xj, axis=1).astype(F32)
            local = dot(bt[j], (weight * xf).astype(BF16))
            if j > 0:
                local = local + decays[j : j + 1, :] * lb[g, j - 1]
            if j < NCH - 1:
                lb[g, j] = local
            else:
                dst[g] = local
            for half in range(2):
                mix = []
                for e in range(2):
                    h = 20 * half + e
                    cq = jnp.broadcast_to(cums[j * CH : (j + 1) * CH, h : h + 1], (CH, CH))
                    ck = cum_t[j, pl.ds(2 * g + h, 1), :]
                    mix.append((jnp.exp2(jnp.minimum(cq - ck, 100.0)) * sc[j]).astype(BF16))
                zero = jnp.zeros_like(xj[half])
                pair = jnp.concatenate(
                    [jnp.where(lane < 64, xj[half], zero), jnp.where(lane < 64, zero, xj[half])],
                    axis=0,
                )
                inner = dot(jnp.concatenate(mix, axis=1), pair)
                lanes = slice(half * 128, half * 128 + 128)
                skip = decays[8:9, lanes]
                out[g, pl.ds(j * CH, CH), lanes] = inner + skip * xj[half].astype(F32)
        cum[...] = pltpu.roll(cums, 126, 1)

        @pl.when(c == 0)
        def _():
            remote(dst.at[g], d0.at[g], d_send.at[g], d_recv.at[g], sib).start()

    def total_copy(g, m):
        return remote(
            tb.at[g], tr.at[m - 1, g], x_send.at[m - 1, g], x_recv.at[m - 1, g], qn[2 * m]
        )

    def chip_total(g):
        @pl.when(c == 1)
        def _():
            remote(dst.at[g], d0.at[g], d_send.at[g], d_recv.at[g], sib).wait_recv()
            tb[g] = (dx[g, 20:21, :] * d0[g] + dst[g]).astype(BF16)
            for m in range(1, 4):
                total_copy(g, m).start()

    def own_state():
        return remote(fd.at[0], zg.at[z], f_send, f_recv, sib)

    def chip_entry(g):
        @pl.when(c == 1)
        def _():
            for m in range(1, 4):
                total_copy(g, m).wait_recv()
            parts = [tr[m, g].astype(F32) for m in range(3)]
            entry = dx[g, 16:17, :] * parts[0] + dx[g, 17:18, :] * parts[1]
            ib[g] = entry + dx[g, 18:19, :] * parts[2]
            remote(ib.at[g], ib.at[g], i_send.at[g], i_recv.at[g], sib).start()
            for half in range(2):
                head = 20 * half + 2 * g
                lanes = slice(half * 128, half * 128 + 128)
                chips = [(head + e) // 10 for e in range(2)]

                @pl.when((chips[0] == x) | (chips[1] == x))
                def _():
                    leaving = dx[g, 9:10, lanes] * tb[g, :, lanes].astype(F32)
                    for m in range(3):
                        leaving += dx[g, 21 + m : 22 + m, lanes] * tr[m, g, :, lanes].astype(F32)
                    turned = leaving.T.reshape(2, 64, 128).astype(BF16)
                    for e in range(2):
                        @pl.when(chips[e] == x)
                        def _():
                            fd[((head + e) // 5) % 2, (head + e) % 5] = turned[e]

            @pl.when(g == 2 + 5 * (x % 2))
            def _():
                own_state().start()

            @pl.when(g == 4 + 5 * (x % 2))
            def _():
                zg[z] = fd[1]

    def late(g):
        spread = expander(g, 256, BF16)

        @pl.when(c == 0)
        def _():
            remote(ib.at[g], ib.at[g], i_send.at[g], i_recv.at[g], sib).wait_recv()
            d0[g] = ib[g]

        @pl.when(c == 1)
        def _():
            d0[g] = d0[g] + dx[g, 19:20, :] * ib[g]

        incoming = d0[g]
        for j in range(NCH):
            entry = dx[g, 4 + j : 5 + j, :] * incoming
            if j > 0:
                entry = entry + lb[g, j - 1]
            carried = dot(cc[j], jnp.concatenate(halves(entry), axis=0))
            carried = carried * dot(ec[pl.ds(j * CH, CH), :], spread)
            full = out[g, pl.ds(j * CH, CH), :] + carried
            out[g, pl.ds(j * CH, CH), :] = full
            square = full * full
            ssq[pl.ds(j * CH, CH), :] += square[:, :128] + square[:, 128:]

    def zroute(m, here):
        heads = [pl.ds(0, 5)] * 6 + [pl.ds(0, 3), pl.ds(3, 2)]
        dz = ([7, 1, 6, 2, 5, 3, 4, 4] if here else [0, 0, 7, 1, 6, 2, 5, 3])[m]
        ref = zg.at[zi[dz], heads[m]]
        return remote(ref, ref, z_send.at[m], z_recv.at[m], zp if m % 2 == 0 else zm)

    def y_copy(dy):
        return remote(ys.at[dy - 1], yr.at[dy], y_send.at[dy - 1], y_recv.at[dy - 1], yn[dy])

    def route(k):
        if k == 0:
            @pl.when(c == 0)
            def _():
                own_state().wait_recv()
        elif k < 5:
            zroute(2 * k - 2, True).wait_recv()
            zroute(2 * k - 1, True).wait_recv()
        if k < 4:
            zroute(2 * k, False).start()
            zroute(2 * k + 1, False).start()
        elif k == 4:
            for dy in range(1, 4):
                ys[dy - 1] = zg[hold[dy] // 4]
                y_copy(dy).start()
            yr[0] = zg[hold[0] // 4]
        else:
            for dy in range(1, 4):
                y_copy(dy).wait_recv()
            fin_ref[...] = yr[(y + 4 - hold[0] % 4) % 4].astype(F32)

    def normed(j):
        rows = pl.ds(j * CH, CH)
        mean = jnp.sum(ssq[rows, :], axis=1, keepdims=True) * (1.0 / D)
        factor = lax.rsqrt(mean + EPS) * valid[pl.ds(HALO + j * CH, CH), :][:, 0:1]
        for g in range(GROUPS):
            for half in range(2):
                tile = g + 10 * half
                gain = vec_ref[22 + tile : 23 + tile, :]
                part = out[g, rows, 128 * half : 128 * half + 128] * factor * gain
                res_ref[rows, 128 * tile : 128 * tile + 128] = part.astype(BF16)


    def body(t, carry):
        for k in range(7):
            s = t - GAP * k
            @pl.when((s >= (0 if k else 2)) & (s < SLOTS))
            def _():
                @pl.when((c == 0) & has(0, s))
                def _():
                    ring_stage(0, s, k)

                @pl.when(c == 1)
                def _():
                    ring_stage(1, s, k)
        s = t - LAG
        @pl.when((s >= 0) & (s < SLOTS))
        def _():
            @pl.when(c == 0)
            def _():
                half = wb.at[1, s]
                remote(half, half, sib_send.at[s], sib_recv.at[s], sib).wait_recv()

            @pl.when((c == 1) & has(0, s))
            def _():
                half = wb.at[0, s]
                remote(half, half, sib_send.at[s], sib_recv.at[s], sib).wait_recv()

        g = s - 2

        @pl.when(g == -1)
        def _():
            prepare()

        @pl.when(g == 0)
        def _():
            link_decays()

        @pl.when((g >= 0) & (g < GROUPS))
        def _():
            group(g)

        @pl.when((g >= TO_TOTAL) & (g < GROUPS + TO_TOTAL))
        def _():
            chip_total(g - TO_TOTAL)

        @pl.when((g >= TO_ENTRY) & (g < GROUPS + TO_ENTRY))
        def _():
            chip_entry(g - TO_ENTRY)

        for k in range(6):
            @pl.when(g == TO_ENTRY + 3 + 2 * c + 5 * (x % 2) + k)
            def _():
                route(k)

        @pl.when((g >= TO_LATE) & (g < GROUPS + TO_LATE))
        def _():
            late(g - TO_LATE)

        for j in range(NCH):
            @pl.when(g == GROUPS + TO_LATE + j)
            def _():
                normed(j)

        return carry

    assemble(0, range(2))
    for s in range(2):
        for core in range(2):
            if core == 1 or s != 1:
                @pl.when(c == core)
                def _():
                    ring_stage(core, s, 0)
    assemble(1, range(2, SLOTS))
    lax.fori_loop(0, LAG + 2 + GROUPS + TO_LATE + 4, body, 0)

    for copies in w_copies:
        for copy in copies[1:]:
            copy.wait_send()
    for dy in range(1, 4):
        y_copy(dy).wait_send()
    for m in range(8):
        zroute(m, False).wait_send()
    for d in range(1, 8):
        remote(ta.at[q], ta.at[q], t_send.at[d - 1], t_recv.at[d - 1], qn[d]).wait_send()

    def drain_slot(s, carry):
        for core in range(2):
            @pl.when((c == core) & has(core, s))
            def _():
                for m in range(12):
                    sent(core, s, m)
                half = wb.at[core, s]
                remote(half, half, sib_send.at[s], sib_recv.at[s], sib).wait_send()
        return carry

    lax.fori_loop(0, SLOTS, drain_slot, 0)

    def drain_group(g, carry):
        @pl.when(c == 0)
        def _():
            remote(dst.at[g], d0.at[g], d_send.at[g], d_recv.at[g], sib).wait_send()

        @pl.when(c == 1)
        def _():
            remote(ib.at[g], ib.at[g], i_send.at[g], i_recv.at[g], sib).wait_send()
            for m in range(1, 4):
                total_copy(g, m).wait_send()
        return carry

    lax.fori_loop(0, GROUPS, drain_group, 0)

    @pl.when(c == 1)
    def _():
        own_state().wait_send()


def on_device(
    tokens, mix_weight, step_weight, conv_weight, conv_bias, step_bias, decay_rate,
    skip_gain, norm_gain, prompt_len, prompt_start, deal,
):
    heads = decay_rate.shape[0]
    gap = jnp.zeros((128 - heads,), F32)
    vec = jnp.concatenate(
        [conv_bias, norm_gain, step_bias, gap, decay_rate, gap, skip_gain, gap, jnp.zeros((384,), F32)]
    ).reshape(48, 128)

    vm, dma = pltpu.VMEM, pltpu.SemaphoreType.DMA
    vspec = pl.BlockSpec(memory_space=pltpu.VMEM)
    sspec = pl.BlockSpec(memory_space=pltpu.SMEM)
    aspec = pl.BlockSpec(memory_space=pl.ANY)
    result, final = pl.pallas_call(
        kernel,
        out_shape=(
            pltpu.VMEM((SPAN, D), BF16),
            pltpu.VMEM((5, 64, 128), F32),
        ),
        in_specs=[aspec, vspec, vspec, vspec, vspec, sspec, sspec, sspec],
        out_specs=(vspec, vspec),
        scratch_shapes=[
            vm((2, SLOTS, 8, 4, 80, 128), BF16),
            vm((2, 16, 1536), BF16),
            vm((8, 16, 1536), BF16),
            vm((SPAN + HALO, D), BF16),
            vm((SPAN + HALO, 128), F32),
            vm((2, SPAN + HALO, 128), F32),
            pltpu.SMEM((4,), jnp.int32),
            vm((GROUPS, SPAN, 256), F32),
            vm((SPAN, 128), F32),
            vm((NCH, 128, CH), F32),
            vm((SPAN, 256), BF16),
            vm((SPAN, 256), BF16),
            vm((NCH, CH, CH), F32),
            vm((NCH, 128, CH), BF16),
            vm((NCH, CH, 256), BF16),
            vm((24, 128), F32),
            vm((GROUPS, 24, 256), F32),
            vm((8, 8, 128), F32),
            vm((GROUPS, 3, 128, 256), F32),
            vm((GROUPS, 128, 256), F32),
            vm((GROUPS, 128, 256), F32),
            vm((GROUPS, 128, 256), BF16),
            vm((3, GROUPS, 128, 256), BF16),
            vm((GROUPS, 128, 256), F32),
            vm((2, 5, 64, 128), BF16),
            vm((8, 5, 64, 128), BF16),
            vm((3, 5, 64, 128), BF16),
            vm((4, 5, 64, 128), BF16),
            vm((SPAN, 128), F32),
            dma((2, 7)), dma((2, 8)), dma((2,)), dma,
            dma((SLOTS, 12)), dma((SLOTS, 12)), dma((SLOTS,)), dma((SLOTS,)),
            dma((7,)), dma((7,)), dma((GROUPS,)), dma((GROUPS,)),
            dma((3, GROUPS)), dma((3, GROUPS)), dma((GROUPS,)), dma((GROUPS,)),
            dma, dma, dma((8,)), dma((8,)), dma((3,)), dma((3,)),
        ],
        compiler_params=pltpu.CompilerParams(
            collective_id=0, has_side_effects=True, vmem_limit_bytes=52 * 1024 * 1024
        ),
    )(tokens[0], mix_weight, step_weight, conv_weight, vec, prompt_len, prompt_start, deal)
    return (result[None], final[None])


def solution(mesh):
    return jax.shard_map(
        on_device,
        mesh=mesh,
        in_specs=(P("req", "seq", None), P(("req", "seq"), None), P(("req", "seq"), None))
        + (P(),) * 9,
        out_specs=(P("req", "seq", None), P("req", "seq", None, None)),
        check_vma=False,
    )
```

```python
import functools

import jax
import jax.numpy as jnp
from jax import lax
from jax.experimental import pallas as pl
from jax.experimental.pallas import tpu as pltpu
from jax.sharding import PartitionSpec as P

F32, BF16 = jnp.float32, jnp.bfloat16
MESH = pl.DeviceIdType.MESH
HIGH = lax.Precision.HIGHEST
EPS = 1e-05

SPAN = 512
HALO = 16
CH = 128
NCH = SPAN // CH
D = 2560
SLOTS = 12
GROUPS = 10
GAP = 2
LAG = 6 * GAP + 1
LOG2E = 1.4426950408889634
TO_TOTAL, TO_ENTRY, TO_LATE = 1, 3, 5


def dot(a, b, **kw):
    return jnp.dot(a, b, preferred_element_type=F32, **kw)


def kernel(
    tok_hbm, mix_ref, sw_ref, cw_ref, cb_ref, ng_ref, sb_ref, dr_ref, sg_ref, len_s, start_s, deal_s,
    res_ref, fin_ref,
    wb, wl_ref, stage, tokv, valid, conv, hold, hv, out, cum, cum_t, wk, ec, sc, bt, cc,
    dcw, dx, ta, lb, dst, d0, tb, tr, ib, fd, zg, ys, yr, ssq,
    w_send, w_recv, h_sem, tok_sem, g_send, g_recv, sib_send, sib_recv,
    t_send, t_recv, d_send, d_recv, x_send, x_recv, i_send, i_recv,
    f_send, f_recv, z_send, z_recv, y_send, y_recv,
):
    r, q = lax.axis_index("req"), lax.axis_index("seq")
    z, y, x, c = r // 4, r % 4, q // 2, q % 2
    yn = [(z * 4 + (y + d) % 4, q) for d in range(4)]
    zn = [(((z + d) % 8) * 4 + y, q) for d in range(8)]
    qn = [(r, (q + d) % 8) for d in range(8)]
    yp, ym, zp, zm = yn[1], yn[3], zn[1], zn[7]
    sib = (r, q + 1 - 2 * c)
    yi = [(y + d) % 4 for d in range(4)]
    zi = [(z + d) % 8 for d in range(8)]

    def remote(src, to, ssem, rsem, dev):
        return pltpu.make_async_remote_copy(
            src_ref=src, dst_ref=to, send_sem=ssem, recv_sem=rsem,
            device_id=dev, device_id_type=MESH,
        )

    barrier = pltpu.get_barrier_semaphore()
    partners = qn[1:] + yn[1:] + [zp, zm]
    for dev in partners:
        pl.semaphore_signal(barrier, inc=1, device_id=dev, device_id_type=MESH)
    tok_copy = pltpu.make_async_copy(tok_hbm, tokv.at[pl.ds(HALO, SPAN)], tok_sem)
    tok_copy.start()
    hv[...] = jnp.zeros_like(hv)
    for n, ref in enumerate((sb_ref, dr_ref, sg_ref)):
        hv[n : n + 1, 0:40] = ref[...]
    wl_ref[...] = jnp.zeros_like(wl_ref)
    wl_ref[0, 0:10, 0:40] = sw_ref[...]
    wl_ref[0, 0:10, 256:1536] = mix_ref[:, 0:1280]
    wl_ref[1, 0:10, 0:256] = mix_ref[:, 2560:2816]
    wl_ref[1, 0:10, 256:1536] = mix_ref[:, 1280:2560]
    pl.semaphore_wait(barrier, len(partners))

    waves = [pl.ds(0, 256), pl.ds(256, 1280)]
    w_copies = []
    for n, cols in enumerate(waves):
        own_w = pltpu.make_async_copy(wl_ref.at[c, :, cols], stage.at[q, :, cols], w_recv.at[n, 7])
        own_w.start()
        w_copies.append([own_w])
        for d in range(1, 8):
            to = (q + d) % 8
            copy = remote(
                wl_ref.at[to % 2, :, cols], stage.at[q, :, cols],
                w_send.at[n, d - 1], w_recv.at[n, d - 1], qn[d],
            )
            copy.start()
            w_copies[n].append(copy)
    halo = remote(
        tok_hbm.at[pl.ds(SPAN - HALO, HALO)], tokv.at[pl.ds(0, HALO)],
        h_sem.at[0], h_sem.at[1], qn[1],
    )
    halo.start()

    def holder(dy):
        target = z * 4 + yi[dy]

        def look(s, found):
            return jnp.where(deal_s[s] == target, s, found)

        return lax.fori_loop(0, 32, look, 0)

    for dy in range(4):
        hold[dy] = holder(dy)
    request = deal_s[r]
    first = start_s[request]
    last = first + len_s[request]
    place = lax.broadcasted_iota(jnp.int32, (SPAN + HALO, 128), 0) + (q * SPAN - HALO)
    valid[...] = jnp.where((place >= first) & (place < last), 1.0, 0.0)
    ssq[...] = jnp.zeros_like(ssq)

    row = lax.broadcasted_iota(jnp.int32, (80, 128), 0)
    col = lax.broadcasted_iota(jnp.int32, (80, 128), 1)
    pick = jnp.where(col == (row // 10) * 16 + row % 10, 1.0, 0.0).astype(BF16)

    def assemble(n, slots):
        w_copies[n][0].wait()
        for d in range(1, 8):
            to = stage.at[(q - d) % 8, :, waves[n]]
            remote(to, to, w_send.at[n, d - 1], w_recv.at[n, d - 1], qn[d]).wait_recv()
        for s in slots:
            part = stage[:, :, s * 128 : (s + 1) * 128].reshape(128, 128)
            wb[c, s, z, y] = dot(pick, part).astype(BF16)

    def blk(s, dz, dy):
        return wb.at[c, s, zi[dz], yi[dy]]

    def lo(ref):
        return ref.at[pl.ds(0, 48)]

    def hi(ref):
        return ref.at[pl.ds(48, 32)]

    def zset(s, dz):
        return wb.at[0, s, zi[dz]]

    def yset(s, dy):
        return wb.at[1, s, :, yi[dy]]

    def messages(core, s):
        if core == 0:
            return [
                (blk(s, 0, 3), blk(s, 0, 0), yp),
                (blk(s, 0, 1), blk(s, 0, 0), ym),
                (lo(blk(s, 0, 2)), lo(blk(s, 0, 3)), yp),
                (hi(blk(s, 0, 2)), hi(blk(s, 0, 1)), ym),
                (zset(s, 7), zset(s, 0), zp),
                (zset(s, 1), zset(s, 0), zm),
                (zset(s, 6), zset(s, 7), zp),
                (zset(s, 2), zset(s, 1), zm),
                (zset(s, 5), zset(s, 6), zp),
                (zset(s, 3), zset(s, 2), zm),
                (zset(s, 4).at[pl.ds(0, 2)], zset(s, 5).at[pl.ds(0, 2)], zp),
                (zset(s, 4).at[pl.ds(2, 2)], zset(s, 3).at[pl.ds(2, 2)], zm),
            ]
        return [
            (blk(s, 7, 0), blk(s, 0, 0), zp),
            (blk(s, 1, 0), blk(s, 0, 0), zm),
            (blk(s, 6, 0), blk(s, 7, 0), zp),
            (blk(s, 2, 0), blk(s, 1, 0), zm),
            (blk(s, 5, 0), blk(s, 6, 0), zp),
            (blk(s, 3, 0), blk(s, 2, 0), zm),
            (lo(blk(s, 4, 0)), lo(blk(s, 5, 0)), zp),
            (hi(blk(s, 4, 0)), hi(blk(s, 3, 0)), zm),
            (yset(s, 3), yset(s, 0), yp),
            (yset(s, 1), yset(s, 0), ym),
            (wb.at[1, s, pl.ds(0, 4), yi[2]], wb.at[1, s, pl.ds(0, 4), yi[3]], yp),
            (wb.at[1, s, pl.ds(4, 4), yi[2]], wb.at[1, s, pl.ds(4, 4), yi[1]], ym),
        ]

    def send(core, s, m):
        _, src, dev = messages(core, s)[m]
        remote(src, src, g_send.at[s, m], g_recv.at[s, m], dev).start()

    def got(core, s, m):
        here, _, dev = messages(core, s)[m]
        remote(here, here, g_send.at[s, m], g_recv.at[s, m], dev).wait_recv()

    def sent(core, s, m):
        _, src, dev = messages(core, s)[m]
        remote(src, src, g_send.at[s, m], g_recv.at[s, m], dev).wait_send()

    def ring_stage(core, s, k):
        if k > 0:
            got(core, s, 2 * k - 2)
            got(core, s, 2 * k - 1)
        if k < 6:
            send(core, s, 2 * k)
            send(core, s, 2 * k + 1)
        else:
            half = wb.at[core, s]
            remote(half, half, sib_send.at[s], sib_recv.at[s], sib).start()

    def has(core, s):
        return (s != 1) if core == 0 else True

    def expander(g, rows, kind):
        i = lax.broadcasted_iota(jnp.int32, (rows, 256), 0)
        j = lax.broadcasted_iota(jnp.int32, (rows, 256), 1)
        head = 2 * g + 20 * (j >> 7) + ((j >> 6) & 1)
        return jnp.where((i & 127) == head, 1.0, 0.0).astype(kind)

    def project(w):
        mixed = dot(tokv[...], w)
        v = valid[...]
        for half in range(2):
            part = mixed[:, half * 128 : half * 128 + 128] * v
            conv[half] = part.astype(BF16).astype(F32)

    def convolve(half, j, tile):
        lanes = pl.ds(pl.multiple_of(tile * 128, 128), 128)
        acc = jnp.broadcast_to(cb_ref[pl.ds(tile, 1), :], (CH, 128))
        for k in range(4):
            acc = acc + cw_ref[k : k + 1, lanes] * conv[half, pl.ds(13 + k + CH * j, CH), :]
        acc = 0.5 * acc
        return (acc + acc * jnp.tanh(acc)).astype(BF16)

    def halves(v):
        top = v.astype(BF16)
        low = (v - top.astype(F32)).astype(BF16)
        return top, low

    ri = lax.broadcasted_iota(jnp.int32, (CH, CH), 0)
    ci = lax.broadcasted_iota(jnp.int32, (CH, CH), 1)

    def prepare():
        tok_copy.wait()
        halo.wait_send()
        halo.wait_recv()
        raw = dot(tokv[pl.ds(HALO, SPAN), :], wb[0, 0].reshape(D, 128))
        project(jnp.concatenate([wb[1, 0].reshape(D, 128), wb[1, 1].reshape(D, 128)], axis=1))
        tri = jnp.where(ri >= ci, 1.0, 0.0)
        before = jnp.zeros((1, 128), F32)
        for j in range(NCH):
            rows = slice(j * CH, (j + 1) * CH)
            b = convolve(0, j, 20)
            cj = convolve(1, j, 21)
            cc[j] = jnp.concatenate([cj, cj], axis=1)
            bt[j] = b.astype(F32).T.astype(BF16)
            score = lax.dot_general(cj, b, (((1,), (1,)), ((), ())), preferred_element_type=F32)
            sc[j] = jnp.where(ri >= ci, score, 0.0)
            v = raw[rows] + hv[0:1, :]
            step = jnp.maximum(v, 0.0) + jnp.log1p(jnp.exp(-jnp.abs(v)))
            step = step * valid[pl.ds(HALO + j * CH, CH), :]
            total = dot(tri, -step * hv[1:2, :], precision=HIGH)
            cum[pl.ds(j * CH, CH), :] = total * LOG2E
            cum_t[j] = ((total - jnp.log(step)) * LOG2E).T
            end = total[CH - 1 : CH, :]
            top, low = halves(jnp.exp(end - total) * step)
            wk[pl.ds(j * CH, CH), :] = jnp.concatenate([top, low], axis=1)
            top, low = halves(jnp.exp(total))
            ec[pl.ds(j * CH, CH), :] = jnp.concatenate([top, low], axis=1)
            dcw[j : j + 1, :] = jnp.exp(end)
            dcw[4 + j : 5 + j, :] = jnp.exp(before)
            before = before + end
        dcw[8:9, :] = hv[2:3, :]
        ta[q] = jnp.broadcast_to(before, (8, 128))
        for d in range(1, 8):
            remote(ta.at[q], ta.at[q], t_send.at[d - 1], t_recv.at[d - 1], qn[d]).start()

    def link_decays():
        for d in range(1, 8):
            src = (q - d) % 8
            remote(ta.at[src], ta.at[src], t_send.at[d - 1], t_recv.at[d - 1], qn[d]).wait_recv()
        tot = [ta[d][0:1, :] for d in range(8)]
        dcw[16:24, :] = jnp.zeros((8, 128), F32)
        def between(lower, upper):
            acc = jnp.zeros((1, 128), F32)
            for d in range(8):
                acc = acc + tot[d] * jnp.where((d >= lower) & (d < upper), 1.0, 0.0)
            return jnp.exp(acc)

        for m in range(1, 4):
            xs = (x - m) % 4
            dcw[15 + m : 16 + m, :] = between(2 * xs + 2, 2 * x) * jnp.where(xs < x, 1.0, 0.0)
            dcw[20 + m : 21 + m, :] = between(2 * xs + 2, 8)
        dcw[9:10, :] = between(2 * x + 2, 8)
        dcw[19:20, :] = jnp.exp(ta[2 * x][0:1, :])
        dcw[20:21, :] = jnp.exp(ta[2 * x + 1][0:1, :])

    lane = lax.broadcasted_iota(jnp.int32, (CH, 128), 1)

    def group(g):
        s = g + 2
        project(jnp.concatenate([wb[0, s].reshape(D, 128), wb[1, s].reshape(D, 128)], axis=1))
        spread = expander(g, 256, BF16)
        decays = dot(dcw[...], expander(g, 128, F32), precision=HIGH)
        dx[g] = decays
        cums = cum[...]
        for j in range(NCH):
            xj = [convolve(half, j, g + 10 * half) for half in range(2)]
            weight = dot(wk[pl.ds(j * CH, CH), :], spread)
            xf = jnp.concatenate(xj, axis=1).astype(F32)
            local = dot(bt[j], (weight * xf).astype(BF16))
            if j > 0:
                local = local + decays[j : j + 1, :] * lb[g, j - 1]
            if j < NCH - 1:
                lb[g, j] = local
            else:
                dst[g] = local
            for half in range(2):
                mix = []
                for e in range(2):
                    h = 20 * half + e
                    cq = jnp.broadcast_to(cums[j * CH : (j + 1) * CH, h : h + 1], (CH, CH))
                    ck = cum_t[j, pl.ds(2 * g + h, 1), :]
                    mix.append((jnp.exp2(jnp.minimum(cq - ck, 100.0)) * sc[j]).astype(BF16))
                zero = jnp.zeros_like(xj[half])
                pair = jnp.concatenate(
                    [jnp.where(lane < 64, xj[half], zero), jnp.where(lane < 64, zero, xj[half])],
                    axis=0,
                )
                inner = dot(jnp.concatenate(mix, axis=1), pair)
                lanes = slice(half * 128, half * 128 + 128)
                skip = decays[8:9, lanes]
                out[g, pl.ds(j * CH, CH), lanes] = inner + skip * xj[half].astype(F32)
        cum[...] = pltpu.roll(cums, 126, 1)

        @pl.when(c == 0)
        def _():
            remote(dst.at[g], d0.at[g], d_send.at[g], d_recv.at[g], sib).start()

    def total_copy(g, m):
        return remote(
            tb.at[g], tr.at[m - 1, g], x_send.at[m - 1, g], x_recv.at[m - 1, g], qn[2 * m]
        )

    def chip_total(g):
        @pl.when(c == 1)
        def _():
            remote(dst.at[g], d0.at[g], d_send.at[g], d_recv.at[g], sib).wait_recv()
            tb[g] = (dx[g, 20:21, :] * d0[g] + dst[g]).astype(BF16)
            for m in range(1, 4):
                total_copy(g, m).start()

    def own_state():
        return remote(fd.at[0], zg.at[z], f_send, f_recv, sib)

    def chip_entry(g):
        @pl.when(c == 1)
        def _():
            for m in range(1, 4):
                total_copy(g, m).wait_recv()
            parts = [tr[m, g].astype(F32) for m in range(3)]
            entry = dx[g, 16:17, :] * parts[0] + dx[g, 17:18, :] * parts[1]
            ib[g] = entry + dx[g, 18:19, :] * parts[2]
            remote(ib.at[g], ib.at[g], i_send.at[g], i_recv.at[g], sib).start()
            for half in range(2):
                head = 20 * half + 2 * g
                lanes = slice(half * 128, half * 128 + 128)
                chips = [(head + e) // 10 for e in range(2)]

                @pl.when((chips[0] == x) | (chips[1] == x))
                def _():
                    leaving = dx[g, 9:10, lanes] * tb[g, :, lanes].astype(F32)
                    for m in range(3):
                        leaving += dx[g, 21 + m : 22 + m, lanes] * tr[m, g, :, lanes].astype(F32)
                    turned = leaving.T.reshape(2, 64, 128).astype(BF16)
                    for e in range(2):
                        @pl.when(chips[e] == x)
                        def _():
                            fd[((head + e) // 5) % 2, (head + e) % 5] = turned[e]

            @pl.when(g == 2 + 5 * (x % 2))
            def _():
                own_state().start()

            @pl.when(g == 4 + 5 * (x % 2))
            def _():
                zg[z] = fd[1]

    def late(g):
        spread = expander(g, 256, BF16)

        @pl.when(c == 0)
        def _():
            remote(ib.at[g], ib.at[g], i_send.at[g], i_recv.at[g], sib).wait_recv()
            d0[g] = ib[g]

        @pl.when(c == 1)
        def _():
            d0[g] = d0[g] + dx[g, 19:20, :] * ib[g]

        incoming = d0[g]
        for j in range(NCH):
            entry = dx[g, 4 + j : 5 + j, :] * incoming
            if j > 0:
                entry = entry + lb[g, j - 1]
            carried = dot(cc[j], jnp.concatenate(halves(entry), axis=0))
            carried = carried * dot(ec[pl.ds(j * CH, CH), :], spread)
            full = out[g, pl.ds(j * CH, CH), :] + carried
            out[g, pl.ds(j * CH, CH), :] = full
            square = full * full
            ssq[pl.ds(j * CH, CH), :] += square[:, :128] + square[:, 128:]

    def zroute(m, here):
        heads = [pl.ds(0, 5)] * 6 + [pl.ds(0, 3), pl.ds(3, 2)]
        dz = ([7, 1, 6, 2, 5, 3, 4, 4] if here else [0, 0, 7, 1, 6, 2, 5, 3])[m]
        ref = zg.at[zi[dz], heads[m]]
        return remote(ref, ref, z_send.at[m], z_recv.at[m], zp if m % 2 == 0 else zm)

    def y_copy(dy):
        return remote(ys.at[dy - 1], yr.at[dy], y_send.at[dy - 1], y_recv.at[dy - 1], yn[dy])

    def route(k):
        if k == 0:
            @pl.when(c == 0)
            def _():
                own_state().wait_recv()
        elif k < 5:
            zroute(2 * k - 2, True).wait_recv()
            zroute(2 * k - 1, True).wait_recv()
        if k < 4:
            zroute(2 * k, False).start()
            zroute(2 * k + 1, False).start()
        elif k == 4:
            for dy in range(1, 4):
                ys[dy - 1] = zg[hold[dy] // 4]
                y_copy(dy).start()
            yr[0] = zg[hold[0] // 4]
        else:
            for dy in range(1, 4):
                y_copy(dy).wait_recv()
            fin_ref[...] = yr[(y + 4 - hold[0] % 4) % 4].astype(F32)

    def normed(j):
        rows = pl.ds(j * CH, CH)
        mean = jnp.sum(ssq[rows, :], axis=1, keepdims=True) * (1.0 / D)
        factor = lax.rsqrt(mean + EPS) * valid[pl.ds(HALO + j * CH, CH), :][:, 0:1]
        for g in range(GROUPS):
            for half in range(2):
                tile = g + 10 * half
                gain = ng_ref[tile : tile + 1, :]
                part = out[g, rows, 128 * half : 128 * half + 128] * factor * gain
                res_ref[rows, 128 * tile : 128 * tile + 128] = part.astype(BF16)


    def body(t, carry):
        for k in range(7):
            s = t - GAP * k
            @pl.when((s >= (0 if k else 2)) & (s < SLOTS))
            def _():
                @pl.when((c == 0) & has(0, s))
                def _():
                    ring_stage(0, s, k)

                @pl.when(c == 1)
                def _():
                    ring_stage(1, s, k)
        s = t - LAG
        @pl.when((s >= 0) & (s < SLOTS))
        def _():
            @pl.when(c == 0)
            def _():
                half = wb.at[1, s]
                remote(half, half, sib_send.at[s], sib_recv.at[s], sib).wait_recv()

            @pl.when((c == 1) & has(0, s))
            def _():
                half = wb.at[0, s]
                remote(half, half, sib_send.at[s], sib_recv.at[s], sib).wait_recv()

        g = s - 2

        @pl.when(g == -1)
        def _():
            prepare()

        @pl.when(g == 0)
        def _():
            link_decays()

        @pl.when((g >= 0) & (g < GROUPS))
        def _():
            group(g)

        @pl.when((g >= TO_TOTAL) & (g < GROUPS + TO_TOTAL))
        def _():
            chip_total(g - TO_TOTAL)

        @pl.when((g >= TO_ENTRY) & (g < GROUPS + TO_ENTRY))
        def _():
            chip_entry(g - TO_ENTRY)

        for k in range(6):
            @pl.when(g == TO_ENTRY + 3 + 2 * c + 5 * (x % 2) + k)
            def _():
                route(k)

        @pl.when((g >= TO_LATE) & (g < GROUPS + TO_LATE))
        def _():
            late(g - TO_LATE)

        for j in range(NCH):
            @pl.when(g == GROUPS + TO_LATE + j)
            def _():
                normed(j)

        return carry

    assemble(0, range(2))
    for s in range(2):
        for core in range(2):
            if core == 1 or s != 1:
                @pl.when(c == core)
                def _():
                    ring_stage(core, s, 0)
    assemble(1, range(2, SLOTS))
    lax.fori_loop(0, LAG + 2 + GROUPS + TO_LATE + 4, body, 0)

    for copies in w_copies:
        for copy in copies[1:]:
            copy.wait_send()
    for dy in range(1, 4):
        y_copy(dy).wait_send()
    for m in range(8):
        zroute(m, False).wait_send()
    for d in range(1, 8):
        remote(ta.at[q], ta.at[q], t_send.at[d - 1], t_recv.at[d - 1], qn[d]).wait_send()

    def drain_slot(s, carry):
        for core in range(2):
            @pl.when((c == core) & has(core, s))
            def _():
                for m in range(12):
                    sent(core, s, m)
                half = wb.at[core, s]
                remote(half, half, sib_send.at[s], sib_recv.at[s], sib).wait_send()
        return carry

    lax.fori_loop(0, SLOTS, drain_slot, 0)

    def drain_group(g, carry):
        @pl.when(c == 0)
        def _():
            remote(dst.at[g], d0.at[g], d_send.at[g], d_recv.at[g], sib).wait_send()

        @pl.when(c == 1)
        def _():
            remote(ib.at[g], ib.at[g], i_send.at[g], i_recv.at[g], sib).wait_send()
            for m in range(1, 4):
                total_copy(g, m).wait_send()
        return carry

    lax.fori_loop(0, GROUPS, drain_group, 0)

    @pl.when(c == 1)
    def _():
        own_state().wait_send()


def on_device(
    tokens, mix_weight, step_weight, conv_weight, conv_bias, step_bias, decay_rate,
    skip_gain, norm_gain, prompt_len, prompt_start, deal,
):
    rows = [conv_bias.reshape(22, 128), norm_gain.reshape(20, 128)]
    rows += [v.reshape(1, 40) for v in (step_bias, decay_rate, skip_gain)]

    vm, dma = pltpu.VMEM, pltpu.SemaphoreType.DMA
    vspec = pl.BlockSpec(memory_space=pltpu.VMEM)
    sspec = pl.BlockSpec(memory_space=pltpu.SMEM)
    aspec = pl.BlockSpec(memory_space=pl.ANY)
    result, final = pl.pallas_call(
        kernel,
        out_shape=(
            pltpu.VMEM((SPAN, D), BF16),
            pltpu.VMEM((5, 64, 128), F32),
        ),
        in_specs=[aspec] + [vspec] * 8 + [sspec, sspec, sspec],
        out_specs=(vspec, vspec),
        scratch_shapes=[
            vm((2, SLOTS, 8, 4, 80, 128), BF16),
            vm((2, 16, 1536), BF16),
            vm((8, 16, 1536), BF16),
            vm((SPAN + HALO, D), BF16),
            vm((SPAN + HALO, 128), F32),
            vm((2, SPAN + HALO, 128), F32),
            pltpu.SMEM((4,), jnp.int32),
            vm((8, 128), F32),
            vm((GROUPS, SPAN, 256), F32),
            vm((SPAN, 128), F32),
            vm((NCH, 128, CH), F32),
            vm((SPAN, 256), BF16),
            vm((SPAN, 256), BF16),
            vm((NCH, CH, CH), F32),
            vm((NCH, 128, CH), BF16),
            vm((NCH, CH, 256), BF16),
            vm((24, 128), F32),
            vm((GROUPS, 24, 256), F32),
            vm((8, 8, 128), F32),
            vm((GROUPS, 3, 128, 256), F32),
            vm((GROUPS, 128, 256), F32),
            vm((GROUPS, 128, 256), F32),
            vm((GROUPS, 128, 256), BF16),
            vm((3, GROUPS, 128, 256), BF16),
            vm((GROUPS, 128, 256), F32),
            vm((2, 5, 64, 128), BF16),
            vm((8, 5, 64, 128), BF16),
            vm((3, 5, 64, 128), BF16),
            vm((4, 5, 64, 128), BF16),
            vm((SPAN, 128), F32),
            dma((2, 7)), dma((2, 8)), dma((2,)), dma,
            dma((SLOTS, 12)), dma((SLOTS, 12)), dma((SLOTS,)), dma((SLOTS,)),
            dma((7,)), dma((7,)), dma((GROUPS,)), dma((GROUPS,)),
            dma((3, GROUPS)), dma((3, GROUPS)), dma((GROUPS,)), dma((GROUPS,)),
            dma, dma, dma((8,)), dma((8,)), dma((3,)), dma((3,)),
        ],
        compiler_params=pltpu.CompilerParams(
            collective_id=0, has_side_effects=True, vmem_limit_bytes=52 * 1024 * 1024
        ),
    )(tokens[0], mix_weight, step_weight, conv_weight, *rows, prompt_len, prompt_start, deal)
    return (result[None], final[None])


def solution(mesh):
    return jax.shard_map(
        on_device,
        mesh=mesh,
        in_specs=(P("req", "seq", None), P(("req", "seq"), None), P(("req", "seq"), None))
        + (P(),) * 9,
        out_specs=(P("req", "seq", None), P("req", "seq", None, None)),
        check_vma=False,
    )
```
